128 devices in a mesh: prompt: 4 (over x), dp: 4 (over y), mp: 8 (over z, core).
Axes of the slice: x: 4, y: 4, z: 4, core: 2. Of those that a mesh axis runs over, the one named last changes fastest.
Arguments:
- prompts: bfloat16 [8, 100, 4096], P('prompt'), may hold values from -6 to 6
- target_embed: bfloat16 [4, 512, 4096], P('dp'), may hold values from -6 to 6
- labels: int32 [4, 512], P('dp'), may hold values from 0 to 16383
- lengths: int32 [4], P('dp'), may hold values from 128 to 512
- attn_gain: float32 [4096], replicated, may hold values from 0.5 to 1.5
- w_qkv: bfloat16 [3, 4096, 2048], P(None, None, 'mp'), may hold values from -4 to 4
- w_out: bfloat16 [2048, 4096], P('mp'), may hold values from -0.5 to 0.5
- final_gain: float32 [4096], replicated, may hold values from 0.5 to 1.5
- w_vocab: bfloat16 [4096, 16384], P(None, ('dp', 'mp')), may hold values from -3 to 3
Outputs:
- token_loss: float32 [8, 4, 512], P('prompt', 'dp')
- prompt_loss: float32 [8], replicated
The draws below stay inside these ranges and needn't reach their ends.
Inputs may be any that keep to these rules, and one draw needn't show every extreme that they name: `lengths`: positions from a sequence's length on are padding.
All inputs are finite; a program needn't handle non-finite values.
Results may differ from the reference program's by a relative error of at most 0.006.
Values may be sent and summed in bfloat16 or wider, within the bound.
No kernel may reach another device: no remote copies, remote signals or barrier semaphores. Data moves between devices by JAX's collectives and lax.ppermute only.
A program may use at most 128 MiB of HBM per device.

```python
import math
import jax
import jax.numpy as jnp
from jax import lax

D = 4096
HEADS = 16
HD = 128
V = 16384
LP = 100
S = 512
P_SIZE = 8
B = 4
N_MP = 8


def draw_w_qkv(key, part):
    noise = jnp.clip(jax.random.normal(key, (3, D, HEADS * HD), jnp.float32), -6.0, 6.0) / math.sqrt(D)
    return jnp.clip(noise, -4.0, 4.0).astype(jnp.bfloat16)


def draw_w_vocab(key, part):
    noise = jnp.clip(jax.random.normal(key, (D, V), jnp.float32), -6.0, 6.0)
    return (noise * 0.0625).astype(jnp.bfloat16)


def with_ends(drawn, own_key, low, top_value):
    spot = [jax.random.randint(jax.random.fold_in(own_key, axis), (), 0, length) for axis, length in enumerate(drawn.shape)]
    widest = drawn.shape.index(max(drawn.shape))
    neighbour = spot[:widest] + [(spot[widest] + 1) % drawn.shape[widest]] + spot[widest + 1:]
    return drawn.at[tuple(spot)].set(low).at[tuple(neighbour)].set(top_value)


def levels(stream_key, extent, cuts, smallest, top_value):
    loudness = 1.0
    for position, parts in cuts:
        heights = jax.random.uniform(jax.random.fold_in(jax.random.fold_in(stream_key, 6), position), (parts,), jnp.float32, smallest / len(cuts), top_value / len(cuts))
        loudness = loudness * jnp.repeat(jnp.exp(heights), extent[position] // parts).reshape((-1,) + (1,) * (len(extent) - 1 - position))
    return loudness


def bell_draw(key, extent, width, bound, split=(), kind=jnp.bfloat16):
    level = levels(key, extent, split, -0.22, 0.18) if split else 1.0
    result = jax.random.normal(key, extent, jnp.float32) * width * level
    return jnp.minimum(jnp.maximum(result, -bound), bound).astype(kind)


def setup_inputs(seed: int = 0) -> dict:
    keys = jax.random.split(jax.random.key(seed), 10)
    prompts = bell_draw(keys[0], (P_SIZE, LP, D), 1.0, 6.0, ((0, 4),))
    target_embed = bell_draw(keys[1], (B, S, D), 1.0, 6.0, ((0, 4),))
    labels = with_ends(jax.random.randint(keys[2], (B, S), 0, V), jax.random.fold_in(keys[2], 1), 0, V - 1).astype(jnp.int32)
    lengths = with_ends(jax.random.randint(keys[3], (B,), S // 4, S + 1), jax.random.fold_in(keys[3], 1), S // 4, S).astype(jnp.int32)
    attn_gain = jnp.clip(1.0 + 0.1 * jax.random.normal(keys[4], (D,), jnp.float32), 0.5, 1.5)
    w_qkv = draw_w_qkv(jax.random.fold_in(keys[9], 71), 0)
    w_out = bell_draw(keys[6], (HEADS * HD, D), (HEADS * HD // 16) ** -0.5, 0.5, ((0, 8),))
    final_gain = jnp.clip(1.0 + 0.1 * jax.random.normal(keys[7], (D,), jnp.float32), 0.5, 1.5)
    w_vocab = draw_w_vocab(jax.random.fold_in(keys[9], 71), 0)
    return {"prompts": prompts, "target_embed": target_embed, "labels": labels, "lengths": lengths, "attn_gain": attn_gain, "w_qkv": w_qkv, "w_out": w_out, "final_gain": final_gain, "w_vocab": w_vocab}


EPSILON = 1e-05
BASE_THETA = 10000.0

def rms_scaled(values, gain_vec):
    widened = values.astype(jnp.float32)
    return widened * lax.rsqrt(lax.optimization_barrier(jnp.mean(widened * widened, axis=-1, keepdims=True)) + EPSILON) * gain_vec

def rotate(values, offset, head_dim):
    number_rows = values.shape[-2]
    full_width = values.shape[-1]
    per_head = values.reshape(values.shape[:-1] + (full_width // head_dim, head_dim))
    half_dim = head_dim // 2
    positions = (offset + jnp.arange(number_rows, dtype=jnp.int32)).astype(jnp.float32)
    indices_f = jnp.arange(half_dim, dtype=jnp.int32).astype(jnp.float32)
    frequency = jnp.exp(indices_f * (-2.0 * math.log(BASE_THETA) / head_dim))
    angles = positions[:, None] * frequency[None, :]
    cosine = jnp.cos(angles)[:, None, :]
    sine_part = jnp.sin(angles)[:, None, :]
    first_half = per_head[..., :half_dim]
    second_half = per_head[..., half_dim:]
    turned = jnp.concatenate([first_half * cosine - second_half * sine_part, second_half * cosine + first_half * sine_part], axis=-1)
    return turned.reshape(values.shape)

def attend(prompt_keys, prompt_vals, target_q, target_k, target_v):
    seq_count = target_q.shape[0]
    target_len = target_q.shape[1]
    prompt_len = prompt_keys.shape[0]
    heads_here = target_q.shape[2] // HD
    keys_all = jnp.concatenate([jnp.broadcast_to(prompt_keys[None], (seq_count,) + prompt_keys.shape), target_k], axis=1)
    vals_all = jnp.concatenate([jnp.broadcast_to(prompt_vals[None], (seq_count,) + prompt_vals.shape), target_v], axis=1)
    query_h = target_q.reshape(seq_count, target_len, heads_here, HD).astype(jnp.float32)
    key_h = keys_all.reshape(seq_count, prompt_len + target_len, heads_here, HD).astype(jnp.float32)
    val_h = vals_all.reshape(seq_count, prompt_len + target_len, heads_here, HD).astype(jnp.float32)
    scores = jnp.einsum('bqhe,bkhe->bhqk', query_h, key_h) * HD ** (-0.5)
    key_index = jnp.arange(prompt_len + target_len, dtype=jnp.int32)
    query_pos = prompt_len + jnp.arange(target_len, dtype=jnp.int32)
    allowed = key_index[None, :] <= query_pos[:, None]
    scores = jnp.where(allowed[None, None], scores, -1e+30)
    top_val = lax.optimization_barrier(jnp.max(scores, axis=-1, keepdims=True))
    expo = jnp.exp(scores - top_val)
    probs = (expo / lax.optimization_barrier(jnp.sum(expo, axis=-1, keepdims=True))).astype(jnp.bfloat16)
    context = jnp.einsum('bhqk,bkhe->bqhe', probs.astype(jnp.float32), val_h)
    return context.astype(jnp.bfloat16).reshape(seq_count, target_len, heads_here * HD)

def reference(prompts, target_embed, labels, lengths, attn_gain, w_qkv, w_out, final_gain, w_vocab):
    seq_count = target_embed.shape[0]
    full_width = w_qkv.shape[2]
    group_width = full_width // N_MP
    normed_target = rms_scaled(target_embed, attn_gain).astype(jnp.bfloat16)
    flat_target = normed_target.reshape(-1, D)

    def linear(rows_in, index_w):
        return jnp.dot(rows_in, w_qkv[index_w], preferred_element_type=jnp.float32).reshape(seq_count, S, full_width)
    target_q = rotate(linear(flat_target, 0), LP, HD).astype(jnp.bfloat16)
    target_k = rotate(linear(flat_target, 1), LP, HD).astype(jnp.bfloat16)
    target_v = linear(flat_target, 2).astype(jnp.bfloat16)
    normed_prompts = rms_scaled(prompts, attn_gain).astype(jnp.bfloat16)
    residual = target_embed.reshape(-1, D).astype(jnp.float32)
    valid = jnp.arange(S, dtype=jnp.int32)[None, :] < lengths[:, None]
    flat_labels = labels.reshape(-1, 1)

    def one_prompt(prompt_rows):
        prompt_k = rotate(jnp.dot(prompt_rows, w_qkv[1], preferred_element_type=jnp.float32), 0, HD).astype(jnp.bfloat16)
        prompt_v = jnp.dot(prompt_rows, w_qkv[2], preferred_element_type=jnp.float32).astype(jnp.bfloat16)
        context = attend(prompt_k, prompt_v, target_q, target_k, target_v)
        ctx_flat = context.reshape(-1, full_width)
        hidden = residual
        for group in range(N_MP):
            part = jnp.dot(ctx_flat[:, group * group_width:(group + 1) * group_width], w_out[group * group_width:(group + 1) * group_width], preferred_element_type=jnp.float32).astype(jnp.bfloat16)
            part = lax.optimization_barrier(part)
            hidden = hidden + part.astype(jnp.float32)
        normed_out = rms_scaled(hidden, final_gain).astype(jnp.bfloat16)
        logits = jnp.dot(normed_out, w_vocab, preferred_element_type=jnp.float32)
        top_val = lax.optimization_barrier(jnp.max(logits, axis=1))
        log_total = top_val + jnp.log(lax.optimization_barrier(jnp.sum(jnp.exp(logits - top_val[:, None]), axis=1)))
        picked = jnp.take_along_axis(logits, flat_labels, axis=1)[:, 0]
        losses = (log_total - picked).reshape(seq_count, S)
        return jnp.where(valid, losses, 0.0)
    token_loss = lax.map(one_prompt, normed_prompts)
    prompt_loss = lax.optimization_barrier(jnp.sum(token_loss, axis=(1, 2))) / jnp.sum(lengths).astype(jnp.float32)
    return (token_loss, prompt_loss)
```

```python
import math

import jax
import jax.numpy as jnp
from jax import lax
from jax.sharding import Mesh
from jax.sharding import PartitionSpec as P

HD = 128
MP = ("mp_0", "mp_1")
DP_MP = ("dp", "mp_0", "mp_1")


EPSILON = 1e-05
BASE_THETA = 10000.0


def of_everyone(value, axis):
    copies = jnp.broadcast_to(value, (lax.axis_size(axis), *value.shape))
    everything = lax.all_to_all(copies, axis, split_axis=0, concat_axis=0, tiled=True)
    return jnp.sum(everything, axis=0)


def shifted(value, axis, shift):
    n = lax.axis_size(axis)
    return lax.ppermute(value, axis, [(i, (i + shift) % n) for i in range(n)])


def ring_of_four(block, axis):
    half = block.shape[0] // 2
    before = shifted(block, axis, 1)
    after = shifted(block, axis, -1)
    far_low = shifted(before[:half], axis, 1)
    far_high = shifted(after[half:], axis, -1)
    return [block, before, after, jnp.concatenate([far_low, far_high], axis=0)]


RING = (0, 3, 1, 2)


def rms_scaled(values, gain_vec):
    widened = values.astype(jnp.float32)
    return (
        widened
        * lax.rsqrt(jnp.mean(widened * widened, axis=-1, keepdims=True) + EPSILON)
        * gain_vec
    )


def rotate(values, offset, head_dim):
    number_rows = values.shape[-2]
    full_width = values.shape[-1]
    per_head = values.reshape(values.shape[:-1] + (full_width // head_dim, head_dim))
    half_dim = head_dim // 2
    positions = (offset + jnp.arange(number_rows, dtype=jnp.int32)).astype(jnp.float32)
    indices_f = jnp.arange(half_dim, dtype=jnp.int32).astype(jnp.float32)
    frequency = jnp.exp(indices_f * (-2.0 * math.log(BASE_THETA) / head_dim))
    angles = positions[:, None] * frequency[None, :]
    cosine = jnp.cos(angles)[:, None, :]
    sine_part = jnp.sin(angles)[:, None, :]
    first_half = per_head[..., :half_dim]
    second_half = per_head[..., half_dim:]
    turned = jnp.concatenate(
        [
            first_half * cosine - second_half * sine_part,
            second_half * cosine + first_half * sine_part,
        ],
        axis=-1,
    )
    return turned.reshape(values.shape)


def project(normed, weights, offset, rotated_count):
    lead_shape = normed.shape[:-1]
    flat_rows = normed.reshape(-1, normed.shape[-1])
    stacked = jnp.einsum("nd,cde->cne", flat_rows, weights, preferred_element_type=jnp.float32)
    stacked = stacked.reshape((weights.shape[0],) + lead_shape + (weights.shape[2],))
    results = []
    for index_w in range(weights.shape[0]):
        product = stacked[index_w]
        if index_w < rotated_count:
            product = rotate(product, offset, HD)
        results.append(product.astype(jnp.bfloat16))
    return tuple(results)


def attend(prompt_keys, prompt_vals, target_q, target_k, target_v):
    seq_count = target_q.shape[0]
    target_len = target_q.shape[1]
    prompt_len = prompt_keys.shape[0]
    heads_here = target_q.shape[2] // HD
    keys_all = jnp.concatenate([prompt_keys[None], target_k], axis=1)
    vals_all = jnp.concatenate([prompt_vals[None], target_v], axis=1)
    query_h = target_q.reshape(seq_count, target_len, heads_here, HD)
    key_h = keys_all.reshape(seq_count, prompt_len + target_len, heads_here, HD)
    val_h = vals_all.reshape(seq_count, prompt_len + target_len, heads_here, HD)
    scores = jnp.einsum(
        "bqhe,bkhe->bhqk", query_h, key_h, preferred_element_type=jnp.float32
    ) * HD ** (-0.5)
    key_index = jnp.arange(prompt_len + target_len, dtype=jnp.int32)
    query_pos = prompt_len + jnp.arange(target_len, dtype=jnp.int32)
    allowed = key_index[None, :] <= query_pos[:, None]
    scores = jnp.where(allowed[None, None], scores, -1e30)
    top_val = jnp.max(scores, axis=-1, keepdims=True)
    expo = jnp.exp(scores - top_val)
    probs = (expo / jnp.sum(expo, axis=-1, keepdims=True)).astype(jnp.bfloat16)
    context = jnp.einsum("bhqk,bkhe->bqhe", probs, val_h, preferred_element_type=jnp.float32)
    return context.astype(jnp.bfloat16).reshape(seq_count, target_len, heads_here * HD)


def shards(prompts, target_embed, labels, lengths, attn_gain, w_qkv, w_out, final_gain, w_vocab):
    n_prompt = lax.axis_size("prompt")
    n_dp = lax.axis_size("dp")
    n_model = lax.axis_size(MP)
    prompts_here = prompts.shape[0]
    prompt_len = prompts.shape[1]
    target_len = target_embed.shape[1]
    model_width = target_embed.shape[2]
    vocab_cols = w_vocab.shape[1]
    heads_width = w_out.shape[0]
    z_index = lax.axis_index("mp_0")
    core = lax.axis_index("mp_1")
    part = model_width // n_model
    places = [((z_index + r) % 4) * 2 + (core + k) % 2 for r in RING for k in range(2)]

    my_places = ((z_index + jnp.take(jnp.array(RING), lax.axis_index("prompt"))) % 4) * 2
    piece = jnp.concatenate(
        [
            lax.dynamic_slice_in_dim(w_vocab, (my_places + (core + k) % 2) * part, part, 0)
            for k in range(2)
        ],
        axis=0,
    )
    vocab_all = lax.all_gather(piece, ("dp", "prompt"), axis=0, tiled=True)
    vocab_all = vocab_all.reshape(n_dp, model_width, vocab_cols)

    out_cols = lax.all_to_all(
        w_out.reshape(heads_width, n_model, part), MP, split_axis=1, concat_axis=0, tiled=True
    ).reshape(n_model * heads_width, part)
    out_cols = jnp.concatenate(
        [lax.dynamic_slice_in_dim(out_cols, p * heads_width, heads_width, 0) for p in places],
        axis=0,
    )

    normed_target = rms_scaled(target_embed, attn_gain).astype(jnp.bfloat16)
    target_q, target_k, target_v = project(normed_target, w_qkv, prompt_len, 2)
    normed_prompts = rms_scaled(prompts, attn_gain).astype(jnp.bfloat16)
    prompt_k, prompt_v = project(normed_prompts, w_qkv[1:], 0, 1)
    contexts = [
        attend(prompt_k[p], prompt_v[p], target_q, target_k, target_v) for p in range(prompts_here)
    ]
    ctx = jnp.concatenate(contexts, axis=0).reshape(prompts_here * target_len, heads_width)

    def whole_row(block):
        blocks = ring_of_four(block, "mp_0")
        return jnp.concatenate(
            [b for mine in blocks for b in (mine, shifted(mine, "mp_1", 1))], axis=1
        )

    ctx_all = whole_row(ctx)
    attn_part = jnp.dot(ctx_all, out_cols, preferred_element_type=jnp.float32)
    my_place = places[0] * part
    residual = lax.dynamic_slice_in_dim(target_embed[0], my_place, part, 1).astype(jnp.float32)
    hidden = residual[None] + attn_part.reshape(prompts_here, target_len, part)
    gain = lax.dynamic_slice_in_dim(final_gain, my_place, part, 0)
    scaled = (hidden * gain).astype(jnp.bfloat16).reshape(prompts_here * target_len, part)
    rows = whole_row(scaled)
    gain_ring = jnp.concatenate(
        [lax.dynamic_slice_in_dim(final_gain, p * part, part, 0) for p in places], axis=0
    )
    unscaled = rows.astype(jnp.float32) / gain_ring
    inverse = lax.rsqrt(jnp.mean(unscaled * unscaled, axis=-1) + EPSILON)

    row_labels = jnp.tile(labels.reshape(-1), prompts_here)
    my_block = lax.axis_index(MP)
    tops, sums, picks = [], [], []
    for d in range(n_dp):
        column_ids = (d * n_model + my_block) * vocab_cols + jnp.arange(vocab_cols, dtype=jnp.int32)
        logits = jnp.dot(rows, vocab_all[d], preferred_element_type=jnp.float32) * inverse[:, None]
        top_val = jnp.max(logits, axis=1)
        tops.append(top_val)
        sums.append(jnp.sum(jnp.exp(logits - top_val[:, None]), axis=1))
        picks.append(
            jnp.sum(jnp.where(column_ids[None, :] == row_labels[:, None], logits, 0.0), axis=1)
        )

    def total(tops, sums):
        top_val = jnp.max(tops, axis=0)
        return top_val + jnp.log(jnp.sum(sums * jnp.exp(tops - top_val), axis=0))

    here = jnp.stack([total(jnp.stack(tops), jnp.stack(sums)), sum(picks)])
    every = lax.all_gather(here, MP)
    log_total = total(every[:, 0], jnp.ones_like(every[:, 0]))
    losses = (log_total - jnp.sum(every[:, 1], axis=0)).reshape(prompts_here, 1, target_len)
    valid = jnp.arange(target_len, dtype=jnp.int32)[None, :] < lengths[:, None]
    token_loss = jnp.where(valid[None], losses, 0.0)
    prompt_sums = jnp.sum(token_loss, axis=(1, 2))
    all_prompts = prompts_here * n_prompt
    slot_ids = lax.axis_index("prompt") * prompts_here + jnp.arange(prompts_here, dtype=jnp.int32)
    placed = jnp.sum(
        jnp.where(
            jnp.arange(all_prompts, dtype=jnp.int32)[:, None] == slot_ids[None, :],
            prompt_sums[None, :],
            0.0,
        ),
        axis=1,
    )
    valid_here = jnp.sum(lengths).astype(jnp.float32).reshape(1)
    totals = of_everyone(jnp.concatenate([placed, valid_here]), ("prompt", "dp"))
    prompt_loss = totals[:all_prompts] * float(n_prompt) / totals[all_prompts]
    return (token_loss, prompt_loss)


def solution(mesh):
    finer = Mesh(
        mesh.devices.reshape(mesh.shape["prompt"], mesh.shape["dp"], 4, 2),
        ("prompt", "dp", "mp_0", "mp_1"),
    )
    return jax.shard_map(
        shards,
        mesh=finer,
        in_specs=(
            P("prompt", None, None),
            P("dp", None, None),
            P("dp", None),
            P("dp"),
            P(),
            P(None, None, MP),
            P(MP, None),
            P(),
            P(None, DP_MP),
        ),
        out_specs=(P("prompt", "dp", None), P()),
        check_vma=False,
    )
```

```python
import math

import jax
import jax.numpy as jnp
from jax import lax
from jax.experimental import pallas as pl
from jax.experimental.pallas import tpu as pltpu
from jax.sharding import Mesh
from jax.sharding import PartitionSpec as P

HD = 128
MP = ("mp_0", "mp_1")
RING = (0, 3, 1, 2)
EPSILON = 1e-05
BASE_THETA = 10000.0
MASKED = -1e30
VMEM_LIMIT = 56 << 20
CHUNKS = (384, 128)


def of_everyone(value, axis):
    copies = jnp.broadcast_to(value, (lax.axis_size(axis), *value.shape))
    everything = lax.all_to_all(copies, axis, split_axis=0, concat_axis=0, tiled=True)
    return jnp.sum(everything, axis=0)


def shifted(value, axis, shift):
    n = lax.axis_size(axis)
    return lax.ppermute(value, axis, [(i, (i + shift) % n) for i in range(n)])


def whole_row(left, right):
    ring = "mp_0"
    left_before = shifted(left, ring, 1)
    right_after = shifted(right, ring, -1)
    right_before = shifted(right, ring, 1)
    left_after = shifted(left, ring, -1)
    left_far = shifted(left_before, ring, 1)
    right_far = shifted(right_after, ring, -1)
    pairs = [
        (left, right),
        (left_before, right_before),
        (left_after, right_after),
        (left_far, right_far),
    ]
    return [b for pair in pairs for b in (*pair, *(shifted(half, "mp_1", 1) for half in pair))]


def rope_tables(number_rows, offset):
    positions = (offset + jnp.arange(number_rows, dtype=jnp.int32)).astype(jnp.float32)
    indices_f = jnp.arange(HD // 2, dtype=jnp.int32).astype(jnp.float32)
    frequency = jnp.exp(indices_f * (-2.0 * math.log(BASE_THETA) / HD))
    angles = positions[:, None] * frequency[None, :]
    cosine, sine = jnp.cos(angles), jnp.sin(angles)
    return jnp.concatenate([cosine, cosine], axis=1), jnp.concatenate([-sine, sine], axis=1)


def attention_kernel(
    target_ref, prompt_ref, gain_ref, w_ref, cos_t, sin_t, cos_p, sin_p, left_ref, right_ref,
    acc_t, acc_p, sq_t, sq_p, q_s, k_s, v_s, kp_s, vp_s,
):
    step = pl.program_id(0)
    n_prompts = prompt_ref.shape[0]

    @pl.when(step == 0)
    def _():
        acc_t[...] = jnp.zeros_like(acc_t)
        acc_p[...] = jnp.zeros_like(acc_p)
        sq_t[...] = jnp.zeros_like(sq_t)
        sq_p[...] = jnp.zeros_like(sq_p)

    gain = gain_ref[...]

    def lanes_of_squares(x):
        square = x * x
        return sum(square[:, i : i + 128] for i in range(0, square.shape[1], 128))

    x = target_ref[0].astype(jnp.float32)
    sq_t[...] += lanes_of_squares(x)
    scaled = (x * gain).astype(jnp.bfloat16)
    for c in range(3):
        acc_t[c] += jnp.dot(scaled, w_ref[c], preferred_element_type=jnp.float32)
    for p in range(n_prompts):
        x = prompt_ref[p].astype(jnp.float32)
        sq_p[p] += lanes_of_squares(x)
        scaled = (x * gain).astype(jnp.bfloat16)
        for c in range(2):
            acc_p[p, c] += jnp.dot(scaled, w_ref[c + 1], preferred_element_type=jnp.float32)

    @pl.when(step == pl.num_programs(0) - 1)
    def _():
        width = pl.num_programs(0) * target_ref.shape[2]
        heads = q_s.shape[1] // HD

        def inverse(square):
            return lax.rsqrt(jnp.sum(square, axis=1, keepdims=True) / width + EPSILON)

        def turned(values, cos, sin):
            return values * cos + pltpu.roll(values, HD // 2, 1) * sin

        scale_t = inverse(sq_t[...])
        for h in range(heads):
            at = slice(h * HD, (h + 1) * HD)
            q_s[:, at] = turned(acc_t[0, :, at] * scale_t, cos_t[...], sin_t[...]).astype(jnp.bfloat16)
            k_s[:, at] = turned(acc_t[1, :, at] * scale_t, cos_t[...], sin_t[...]).astype(jnp.bfloat16)
            v_s[:, at] = (acc_t[2, :, at] * scale_t).astype(jnp.bfloat16)
            for p in range(n_prompts):
                scale_p = inverse(sq_p[p])
                kp_s[p, :, at] = turned(
                    acc_p[p, 0, :, at] * scale_p, cos_p[...], sin_p[...]
                ).astype(jnp.bfloat16)
                vp_s[p, :, at] = (acc_p[p, 1, :, at] * scale_p).astype(jnp.bfloat16)
        target_len = q_s.shape[0]
        tile = target_len // 2
        transposed = (((1,), (1,)), ((), ()))
        for p in range(n_prompts):
            for h in range(heads):
                at = slice(h * HD, (h + 1) * HD)
                for first in range(0, target_len, tile):
                    seen = first + tile
                    q = q_s[first:seen, at]
                    near = lax.dot_general(
                        q, kp_s[p, :, at], transposed, preferred_element_type=jnp.float32
                    ) * HD ** (-0.5)
                    own = lax.dot_general(
                        q, k_s[:seen, at], transposed, preferred_element_type=jnp.float32
                    ) * HD ** (-0.5)
                    row = first + lax.broadcasted_iota(jnp.int32, own.shape, 0)
                    key = lax.broadcasted_iota(jnp.int32, own.shape, 1)
                    own = jnp.where(key <= row, own, MASKED)
                    top = jnp.maximum(
                        jnp.max(near, axis=1, keepdims=True), jnp.max(own, axis=1, keepdims=True)
                    )
                    near = jnp.exp(near - top)
                    own = jnp.exp(own - top)
                    norm = 1.0 / (
                        jnp.sum(near, axis=1, keepdims=True) + jnp.sum(own, axis=1, keepdims=True)
                    )
                    context = jnp.dot(
                        (near * norm).astype(jnp.bfloat16),
                        vp_s[p, :, at],
                        preferred_element_type=jnp.float32,
                    ) + jnp.dot(
                        (own * norm).astype(jnp.bfloat16),
                        v_s[:seen, at],
                        preferred_element_type=jnp.float32,
                    )
                    out_ref = (left_ref, right_ref)[h]
                    out_ref[p * target_len + first : p * target_len + seen, :] = context.astype(
                        jnp.bfloat16
                    )


def attention(target_embed, prompts, attn_gain, w_qkv):
    n_prompts, prompt_len, width = prompts.shape
    target_len = target_embed.shape[1]
    inner = w_qkv.shape[2]
    chunk = 512
    tables = (*rope_tables(target_len, prompt_len), *rope_tables(prompt_len, 0))
    whole = lambda shape: pl.BlockSpec(shape, lambda k: (0,) * len(shape))
    rows = n_prompts * target_len
    return pl.pallas_call(
        attention_kernel,
        out_shape=[jax.ShapeDtypeStruct((rows, inner // 2), jnp.bfloat16)] * 2,
        grid=(width // chunk,),
        in_specs=[
            pl.BlockSpec((1, target_len, chunk), lambda k: (0, 0, k)),
            pl.BlockSpec((n_prompts, prompt_len, chunk), lambda k: (0, 0, k)),
            pl.BlockSpec((1, chunk), lambda k: (0, k)),
            pl.BlockSpec((3, chunk, inner), lambda k: (0, k, 0)),
            *(whole(t.shape) for t in tables),
        ],
        out_specs=[whole((rows, inner // 2))] * 2,
        scratch_shapes=[
            pltpu.VMEM((3, target_len, inner), jnp.float32),
            pltpu.VMEM((n_prompts, 2, prompt_len, inner), jnp.float32),
            pltpu.VMEM((target_len, 128), jnp.float32),
            pltpu.VMEM((n_prompts, prompt_len, 128), jnp.float32),
            *(pltpu.VMEM((target_len, inner), jnp.bfloat16) for _ in range(3)),
            *(pltpu.VMEM((n_prompts, prompt_len, inner), jnp.bfloat16) for _ in range(2)),
        ],
        compiler_params=pltpu.CompilerParams(vmem_limit_bytes=VMEM_LIMIT),
        cost_estimate=pl.CostEstimate(
            flops=8 * 10**9, bytes_accessed=12 * 10**6, transcendentals=2 * 10**6
        ),
        name="attention",
    )(target_embed, prompts, attn_gain.reshape(1, -1), w_qkv, *tables)


def output_kernel(places_ref, *refs):
    *ctx_refs, w_ref, embed_ref, gain_ref, left_ref, right_ref, ctx_s, w_s = refs
    width = w_ref.shape[1]
    at = 0
    for ref in ctx_refs:
        ctx_s[:, at : at + ref.shape[1]] = ref[...]
        at += ref.shape[1]

    @pl.when(pl.program_id(0) == 0)
    def _():
        for group in range(w_ref.shape[0]):
            w_s[group * width : (group + 1) * width, :] = w_ref[places_ref[group]]

    total = embed_ref[0].astype(jnp.float32) + jnp.dot(
        ctx_s[...], w_s[...], preferred_element_type=jnp.float32
    )
    scaled = (total * gain_ref[...]).astype(jnp.bfloat16)
    half = scaled.shape[1] // 2
    left_ref[...] = scaled[:, :half]
    right_ref[...] = scaled[:, half:]


def output_part(places, contexts, out_cols, target_embed, final_gain):
    rows = contexts[0].shape[0]
    groups, group_width, part = out_cols.shape
    target_len = target_embed.shape[1]
    return pl.pallas_call(
        output_kernel,
        out_shape=[jax.ShapeDtypeStruct((rows, part // 2), jnp.bfloat16)] * 2,
        grid_spec=pltpu.PrefetchScalarGridSpec(
            num_scalar_prefetch=1,
            grid=(rows // target_len,),
            in_specs=[
                *(pl.BlockSpec((target_len, c.shape[1]), lambda i, at: (i, 0)) for c in contexts),
                pl.BlockSpec(out_cols.shape, lambda i, at: (0, 0, 0)),
                pl.BlockSpec((1, target_len, part), lambda i, at: (0, 0, at[0])),
                pl.BlockSpec((1, part), lambda i, at: (0, at[0])),
            ],
            out_specs=[pl.BlockSpec((target_len, part // 2), lambda i, at: (i, 0))] * 2,
            scratch_shapes=[
                pltpu.VMEM((target_len, groups * group_width), jnp.bfloat16),
                pltpu.VMEM((groups * group_width, part), jnp.bfloat16),
            ],
        ),
        compiler_params=pltpu.CompilerParams(vmem_limit_bytes=VMEM_LIMIT),
        cost_estimate=pl.CostEstimate(
            flops=2 * 10**9, bytes_accessed=8 * 10**6, transcendentals=0
        ),
        name="output_part",
    )(places, *contexts, out_cols, target_embed, final_gain.reshape(1, -1))


def vocab_kernel(first_ref, *refs, n_rows, at_column, per_vocab, last):
    row_refs, refs = refs[:n_rows], refs[n_rows:]
    if at_column:
        prior_ref, refs = refs[0], refs[1:]
    degain_ref, label_ref, w_ref, out_ref, rows_s, top_s, sum_s, pick_s, scale_s = refs
    step, tile_id = pl.program_id(0), pl.program_id(1)
    tile = rows_s.shape[0]
    at = pl.ds(pl.multiple_of(tile_id * tile, tile), tile)
    blocks, _, columns = w_ref.shape

    k = 0
    for ref in row_refs:
        rows_s[:, k : k + ref.shape[1]] = ref[...]
        k += ref.shape[1]

    @pl.when(step == 0)
    def _():
        if at_column:
            top_s[at, :] = prior_ref[at, 0:1]
            sum_s[at, :] = jnp.ones((tile, 1), jnp.float32)
            pick_s[at, :] = prior_ref[at, 1:2]
            scale_s[at, :] = prior_ref[at, 2:3]
        else:
            top_s[at, :] = jnp.full((tile, 1), MASKED, jnp.float32)
            sum_s[at, :] = jnp.zeros((tile, 1), jnp.float32)
            pick_s[at, :] = jnp.zeros((tile, 1), jnp.float32)
            squares = jnp.zeros((tile, 128), jnp.float32)
            for i in range(0, rows_s.shape[1], 128):
                x = rows_s[:, i : i + 128].astype(jnp.float32) * degain_ref[:, i : i + 128]
                squares += x * x
            mean = jnp.sum(squares, axis=1, keepdims=True) / rows_s.shape[1]
            scale_s[at, :] = lax.rsqrt(mean + EPSILON)

    weights = jnp.concatenate([w_ref[i] for i in range(blocks)], axis=1)
    logits = jnp.dot(rows_s[...], weights, preferred_element_type=jnp.float32) * scale_s[at, :]
    lane = lax.broadcasted_iota(jnp.int32, (1, blocks * columns), 1)
    column = first_ref[0] + at_column + step * blocks * per_vocab
    column = column + (lane // columns) * per_vocab + lane % columns
    old = top_s[at, :]
    top = jnp.maximum(old, jnp.max(logits, axis=1, keepdims=True))
    sum_s[at, :] = sum_s[at, :] * jnp.exp(old - top) + jnp.sum(
        jnp.exp(logits - top), axis=1, keepdims=True
    )
    pick_s[at, :] += jnp.sum(
        jnp.where(column == label_ref[at, :], logits, 0.0), axis=1, keepdims=True
    )
    top_s[at, :] = top

    @pl.when(step == pl.num_programs(0) - 1)
    def _():
        total = top_s[at, :] + jnp.log(sum_s[at, :])
        lane = lax.broadcasted_iota(jnp.int32, (tile, 128), 1)
        three = jnp.where(lane == 0, total, jnp.where(lane == 1, pick_s[at, :], scale_s[at, :]))
        if last:
            out_ref[...] = three.T[:8, :]
        else:
            out_ref[...] = three


def vocab_stats(first, row_blocks, degain, row_labels, chunk, at_column, per_vocab, prior, last):
    rows = row_blocks[0].shape[0]
    n_blocks, width, columns = chunk.shape
    together = max(1, min(n_blocks, 768 // columns))
    tile = 512
    whole = lambda a: pl.BlockSpec(a.shape, lambda j, i, f: (0, 0))
    priors = [] if prior is None else [prior]
    kernel = lambda *refs: vocab_kernel(
        *refs, n_rows=len(row_blocks), at_column=at_column, per_vocab=per_vocab, last=last
    )
    final_tile = n_blocks // together - 1
    held = lambda j, i: jnp.where(j == final_tile, i, 0)
    return pl.pallas_call(
        kernel,
        out_shape=jax.ShapeDtypeStruct((8, rows) if last else (rows, 128), jnp.float32),
        grid_spec=pltpu.PrefetchScalarGridSpec(
            num_scalar_prefetch=1,
            grid=(n_blocks // together, rows // tile),
            in_specs=[
                *(pl.BlockSpec((tile, b.shape[1]), lambda j, i, f: (i, 0)) for b in row_blocks),
                *(whole(p) for p in priors),
                whole(degain),
                whole(row_labels),
                pl.BlockSpec((together, width, columns), lambda j, i, f: (j, 0, 0)),
            ],
            out_specs=pl.BlockSpec((8, tile), lambda j, i, f: (0, held(j, i)))
            if last
            else pl.BlockSpec((tile, 128), lambda j, i, f: (held(j, i), 0)),
            scratch_shapes=[
                pltpu.VMEM((tile, width), jnp.bfloat16),
                *(pltpu.VMEM((rows, 1), jnp.float32) for _ in range(4)),
            ],
        ),
        compiler_params=pltpu.CompilerParams(vmem_limit_bytes=VMEM_LIMIT),
        cost_estimate=pl.CostEstimate(
            flops=2 * rows * width * n_blocks * columns,
            bytes_accessed=rows * width * 2 + n_blocks * width * columns * 2,
            transcendentals=rows * n_blocks * columns,
        ),
        name="vocab_stats",
    )(first, *row_blocks, *priors, degain, row_labels, chunk)


def pieces_kernel(pair_ref, w_ref, *out_refs):
    at = 0
    for ref in out_refs:
        ref[...] = w_ref[:, at : at + ref.shape[1]]
        at += ref.shape[1]


def vocab_pieces(pair, w_vocab, part):
    return pl.pallas_call(
        pieces_kernel,
        out_shape=[jax.ShapeDtypeStruct((2 * part, c), w_vocab.dtype) for c in CHUNKS],
        grid_spec=pltpu.PrefetchScalarGridSpec(
            num_scalar_prefetch=1,
            grid=(2,),
            in_specs=[pl.BlockSpec((part, w_vocab.shape[1]), lambda i, pair: (pair[i], 0))],
            out_specs=[pl.BlockSpec((part, c), lambda i, pair: (i, 0)) for c in CHUNKS],
        ),
        cost_estimate=pl.CostEstimate(flops=0, bytes_accessed=2 << 20, transcendentals=0),
        name="vocab_pieces",
    )(pair, w_vocab)


def split_kernel(w_ref, out_ref):
    part = out_ref.shape[2]
    for i in range(out_ref.shape[0]):
        out_ref[i] = w_ref[:, i * part : (i + 1) * part]


def split_columns(w, n):
    rows, columns = w.shape
    part = columns // n
    return pl.pallas_call(
        split_kernel,
        out_shape=jax.ShapeDtypeStruct((n, rows, part), w.dtype),
        grid=(2,),
        in_specs=[pl.BlockSpec((rows, columns // 2), lambda i: (0, i))],
        out_specs=pl.BlockSpec((n // 2, rows, part), lambda i: (i, 0, 0)),
        cost_estimate=pl.CostEstimate(flops=0, bytes_accessed=4 << 20, transcendentals=0),
        name="split_columns",
    )(w)


def shards(prompts, target_embed, labels, lengths, attn_gain, w_qkv, w_out, final_gain, w_vocab):
    n_prompt = lax.axis_size("prompt")
    n_dp = lax.axis_size("dp")
    n_model = lax.axis_size(MP)
    prompts_here = prompts.shape[0]
    target_len = target_embed.shape[1]
    model_width = target_embed.shape[2]
    vocab_cols = w_vocab.shape[1]
    heads_width = w_out.shape[0]
    z_index = lax.axis_index("mp_0")
    core = lax.axis_index("mp_1")
    part = model_width // n_model
    places = [((z_index + r) % 4) * 2 + (core + k) % 2 for r in RING for k in range(2)]

    x_index = lax.axis_index("prompt")
    turn = jnp.where(x_index == 0, 0, jnp.where(x_index == 1, 3, x_index - 1))
    my_pair = ((z_index + turn) % 4) * 2
    pair = jnp.stack([my_pair + core, my_pair + 1 - core]).astype(jnp.int32)
    chunks = [
        lax.all_gather(p, ("dp", "prompt"), axis=0, tiled=True).reshape(n_dp, model_width, -1)
        for p in vocab_pieces(pair, w_vocab, part)
    ]

    out_cols = lax.all_to_all(
        split_columns(w_out, n_model), MP, split_axis=0, concat_axis=0, tiled=True
    )

    halves = attention(target_embed, prompts, attn_gain, w_qkv)
    place_ids = jnp.stack(places).astype(jnp.int32)
    halves = output_part(place_ids, whole_row(*halves), out_cols, target_embed, final_gain)
    row_blocks = whole_row(*halves)

    degain = 1.0 / jnp.concatenate(
        [lax.dynamic_slice_in_dim(final_gain, p * part, part, 0) for p in places], axis=0
    ).reshape(1, -1)
    row_labels = jnp.tile(labels.reshape(-1, 1), (prompts_here, 1))
    first = (lax.axis_index(MP) * vocab_cols).astype(jnp.int32).reshape(1)
    here, at_column = None, 0
    for i, chunk in enumerate(chunks):
        here = vocab_stats(
            first, row_blocks, degain, row_labels, chunk, at_column, n_model * vocab_cols, here,
            i == len(chunks) - 1,
        )
        at_column += CHUNKS[i]
    here = here[:2]

    every = lax.all_gather(here, MP)
    top_val = jnp.max(every[:, 0], axis=0)
    log_total = top_val + jnp.log(jnp.sum(jnp.exp(every[:, 0] - top_val), axis=0))
    losses = (log_total - jnp.sum(every[:, 1], axis=0)).reshape(prompts_here, 1, target_len)
    valid = jnp.arange(target_len, dtype=jnp.int32)[None, :] < lengths[:, None]
    token_loss = jnp.where(valid[None], losses, 0.0)
    prompt_sums = jnp.sum(token_loss, axis=(1, 2))
    all_prompts = prompts_here * n_prompt
    slot_ids = lax.axis_index("prompt") * prompts_here + jnp.arange(prompts_here, dtype=jnp.int32)
    placed = jnp.sum(
        jnp.where(
            jnp.arange(all_prompts, dtype=jnp.int32)[:, None] == slot_ids[None, :],
            prompt_sums[None, :],
            0.0,
        ),
        axis=1,
    )
    valid_here = jnp.sum(lengths).astype(jnp.float32).reshape(1)
    totals = of_everyone(jnp.concatenate([placed, valid_here]), ("prompt", "dp"))
    prompt_loss = totals[:all_prompts] * float(n_prompt) / totals[all_prompts]
    return (token_loss, prompt_loss)


def solution(mesh):
    finer = Mesh(
        mesh.devices.reshape(mesh.shape["prompt"], mesh.shape["dp"], 4, 2),
        ("prompt", "dp", "mp_0", "mp_1"),
    )
    return jax.shard_map(
        shards,
        mesh=finer,
        in_specs=(
            P("prompt", None, None),
            P("dp", None, None),
            P("dp", None),
            P("dp"),
            P(),
            P(None, None, MP),
            P(MP, None),
            P(),
            P(None, ("dp", "mp_0", "mp_1")),
        ),
        out_specs=(P("prompt", "dp", None), P()),
        check_vma=False,
    )
```

```python
import math

import jax
import jax.numpy as jnp
import numpy as np
from jax import lax
from jax.experimental import pallas as pl
from jax.experimental.pallas import tpu as pltpu
from jax.sharding import Mesh
from jax.sharding import PartitionSpec as P

HD = 128
MP = ("mp_0", "mp_1")
RING = (0, 3, 1, 2)
EPSILON = 1e-05
BASE_THETA = 10000.0
MASKED = -1e30
VMEM_LIMIT = 56 << 20
LOG2E = math.log2(math.e)


def of_everyone(value, axis):
    copies = jnp.broadcast_to(value, (lax.axis_size(axis), *value.shape))
    everything = lax.all_to_all(copies, axis, split_axis=0, concat_axis=0, tiled=True)
    return jnp.sum(everything, axis=0)


def shifted(value, axis, shift):
    n = lax.axis_size(axis)
    return lax.ppermute(value, axis, [(i, (i + shift) % n) for i in range(n)])


def ring_pairs(left, right, axis):
    left_before = shifted(left, axis, 1)
    right_after = shifted(right, axis, -1)
    right, left_before, right_after = lax.optimization_barrier((right, left_before, right_after))
    left_far = shifted(left_before, axis, 1)
    right_far = shifted(right_after, axis, -1)
    right_before = shifted(right, axis, 1)
    left_after = shifted(left, axis, -1)
    return [
        (left, right),
        (left_before, right_before),
        (left_after, right_after),
        (left_far, right_far),
    ]


def whole_row(left, right):
    pairs = ring_pairs(left, right, "mp_0")
    return [b for pair in pairs for b in (*pair, *(shifted(half, "mp_1", 1) for half in pair))]


def rope_tables(number_rows, offset):
    positions = np.arange(offset, offset + number_rows, dtype=np.float32)
    indices_f = np.arange(HD // 2, dtype=np.float32)
    frequency = np.exp(indices_f * np.float32(-2.0 * math.log(BASE_THETA) / HD))
    angles = positions[:, None] * frequency[None, :]
    return jnp.asarray(np.cos(angles)), jnp.asarray(np.sin(angles))


def attention_kernel(
    target_ref, prompt_ref, gain_ref, w_ref, cos_t, sin_t, cos_p, sin_p, left_ref, right_ref,
    acc_t, acc_p, sq_t, sq_p, q_s, k_s, v_s, kp_s, vp_s,
):
    step = pl.program_id(0)
    n_prompts = prompt_ref.shape[0]

    @pl.when(step == 0)
    def _():
        acc_t[...] = jnp.zeros_like(acc_t)
        acc_p[...] = jnp.zeros_like(acc_p)
        sq_t[...] = jnp.zeros_like(sq_t)
        sq_p[...] = jnp.zeros_like(sq_p)

    gain = gain_ref[...]

    def lanes_of_squares(x):
        square = x * x
        return sum(square[:, i : i + 128] for i in range(0, square.shape[1], 128))

    x = target_ref[0].astype(jnp.float32)
    sq_t[...] += lanes_of_squares(x)
    scaled = (x * gain).astype(jnp.bfloat16)
    for c in range(3):
        acc_t[c] += jnp.dot(scaled, w_ref[c], preferred_element_type=jnp.float32)
    for p in range(n_prompts):
        x = prompt_ref[p].astype(jnp.float32)
        sq_p[p] += lanes_of_squares(x)
        scaled = (x * gain).astype(jnp.bfloat16)
        for c in range(2):
            acc_p[p, c] += jnp.dot(scaled, w_ref[c + 1], preferred_element_type=jnp.float32)

    @pl.when(step == pl.num_programs(0) - 1)
    def _():
        width = pl.num_programs(0) * target_ref.shape[2]
        heads = q_s.shape[1] // HD

        def inverse(square):
            return lax.rsqrt(jnp.sum(square, axis=1, keepdims=True) / width + EPSILON)

        def turned(values, cos, sin):
            cos = jnp.concatenate([cos, cos], axis=1)
            sin = jnp.concatenate([-sin, sin], axis=1)
            return values * cos + pltpu.roll(values, HD // 2, 1) * sin

        scale_t = inverse(sq_t[...])
        for h in range(heads):
            at = slice(h * HD, (h + 1) * HD)
            q_s[:, at] = turned(acc_t[0, :, at] * scale_t, cos_t[...], sin_t[...]).astype(jnp.bfloat16)
            k_s[:, at] = turned(acc_t[1, :, at] * scale_t, cos_t[...], sin_t[...]).astype(jnp.bfloat16)
            v_s[:, at] = (acc_t[2, :, at] * scale_t).astype(jnp.bfloat16)
            for p in range(n_prompts):
                scale_p = inverse(sq_p[p])
                kp_s[p, :, at] = turned(
                    acc_p[p, 0, :, at] * scale_p, cos_p[...], sin_p[...]
                ).astype(jnp.bfloat16)
                vp_s[p, :, at] = (acc_p[p, 1, :, at] * scale_p).astype(jnp.bfloat16)
        target_len = q_s.shape[0]
        tile = target_len // 2
        transposed = (((1,), (1,)), ((), ()))
        def one_prompt(p, carry):
            for h in range(heads):
                at = slice(h * HD, (h + 1) * HD)
                for first in range(0, target_len, tile):
                    seen = first + tile
                    q = q_s[first:seen, at]
                    near = lax.dot_general(
                        q, kp_s[p, :, at], transposed, preferred_element_type=jnp.float32
                    ) * HD ** (-0.5)
                    own = lax.dot_general(
                        q, k_s[:seen, at], transposed, preferred_element_type=jnp.float32
                    ) * HD ** (-0.5)
                    row = first + lax.broadcasted_iota(jnp.int32, own.shape, 0)
                    key = lax.broadcasted_iota(jnp.int32, own.shape, 1)
                    own = jnp.where(key <= row, own, MASKED)
                    top = jnp.maximum(
                        jnp.max(near, axis=1, keepdims=True), jnp.max(own, axis=1, keepdims=True)
                    )
                    near = jnp.exp(near - top)
                    own = jnp.exp(own - top)
                    norm = 1.0 / (
                        jnp.sum(near, axis=1, keepdims=True) + jnp.sum(own, axis=1, keepdims=True)
                    )
                    context = jnp.dot(
                        (near * norm).astype(jnp.bfloat16),
                        vp_s[p, :, at],
                        preferred_element_type=jnp.float32,
                    ) + jnp.dot(
                        (own * norm).astype(jnp.bfloat16),
                        v_s[:seen, at],
                        preferred_element_type=jnp.float32,
                    )
                    out_ref = (left_ref, right_ref)[h]
                    rows = pl.ds(pl.multiple_of(p * target_len + first, tile), tile)
                    out_ref[rows, :] = context.astype(jnp.bfloat16)
            return carry

        lax.fori_loop(0, n_prompts, one_prompt, 0)


def attention(target_embed, prompts, attn_gain, w_qkv):
    n_prompts, prompt_len, width = prompts.shape
    target_len = target_embed.shape[1]
    inner = w_qkv.shape[2]
    chunk = 512
    tables = (*rope_tables(target_len, prompt_len), *rope_tables(prompt_len, 0))
    whole = lambda shape: pl.BlockSpec(shape, lambda k: (0,) * len(shape))
    rows = n_prompts * target_len
    return pl.pallas_call(
        attention_kernel,
        out_shape=[jax.ShapeDtypeStruct((rows, inner // 2), jnp.bfloat16)] * 2,
        grid=(width // chunk,),
        in_specs=[
            pl.BlockSpec((1, target_len, chunk), lambda k: (0, 0, k)),
            pl.BlockSpec((n_prompts, prompt_len, chunk), lambda k: (0, 0, k)),
            pl.BlockSpec((1, chunk), lambda k: (0, k)),
            pl.BlockSpec((3, chunk, inner), lambda k: (0, k, 0)),
            *(whole(t.shape) for t in tables),
        ],
        out_specs=[whole((rows, inner // 2))] * 2,
        scratch_shapes=[
            pltpu.VMEM((3, target_len, inner), jnp.float32),
            pltpu.VMEM((n_prompts, 2, prompt_len, inner), jnp.float32),
            pltpu.VMEM((target_len, 128), jnp.float32),
            pltpu.VMEM((n_prompts, prompt_len, 128), jnp.float32),
            *(pltpu.VMEM((target_len, inner), jnp.bfloat16) for _ in range(3)),
            *(pltpu.VMEM((n_prompts, prompt_len, inner), jnp.bfloat16) for _ in range(2)),
        ],
        compiler_params=pltpu.CompilerParams(vmem_limit_bytes=VMEM_LIMIT),
        cost_estimate=pl.CostEstimate(
            flops=8 * 10**9, bytes_accessed=12 * 10**6, transcendentals=2 * 10**6
        ),
        name="attention",
    )(target_embed, prompts, attn_gain.reshape(1, -1), w_qkv, *tables)


def output_kernel(places_ref, *refs):
    *ctx_refs, w_ref, embed_ref, gain_ref, left_ref, right_ref, ctx_s = refs
    at = 0
    for ref in ctx_refs:
        ctx_s[:, at : at + ref.shape[1]] = ref[...]
        at += ref.shape[1]

    total = embed_ref[0].astype(jnp.float32) + jnp.dot(
        ctx_s[...], w_ref[...], preferred_element_type=jnp.float32
    )
    scaled = (total * gain_ref[...]).astype(jnp.bfloat16)
    half = scaled.shape[1] // 2
    left_ref[...] = scaled[:, :half]
    right_ref[...] = scaled[:, half:]


def output_part(place, contexts, out_cols, target_embed, final_gain):
    rows = contexts[0].shape[0]
    inner, part = out_cols.shape
    target_len = target_embed.shape[1]
    tile = target_len // 2
    return pl.pallas_call(
        output_kernel,
        out_shape=[jax.ShapeDtypeStruct((rows, part // 2), jnp.bfloat16)] * 2,
        grid_spec=pltpu.PrefetchScalarGridSpec(
            num_scalar_prefetch=1,
            grid=(rows // tile,),
            in_specs=[
                *(pl.BlockSpec((tile, c.shape[1]), lambda i, at: (i, 0)) for c in contexts),
                pl.BlockSpec(out_cols.shape, lambda i, at: (0, 0)),
                pl.BlockSpec((1, tile, part), lambda i, at: (0, i % 2, at[0])),
                pl.BlockSpec((1, part), lambda i, at: (0, at[0])),
            ],
            out_specs=[pl.BlockSpec((tile, part // 2), lambda i, at: (i, 0))] * 2,
            scratch_shapes=[pltpu.VMEM((tile, inner), jnp.bfloat16)],
        ),
        compiler_params=pltpu.CompilerParams(vmem_limit_bytes=VMEM_LIMIT),
        cost_estimate=pl.CostEstimate(
            flops=2 * 10**9, bytes_accessed=8 * 10**6, transcendentals=0
        ),
        name="output_part",
    )(place, *contexts, out_cols, target_embed, final_gain.reshape(1, -1))


def assemble_kernel(*refs):
    *row_refs, degain_ref, rows_ref, scale_ref = refs
    tile, width = rows_ref.shape
    squares = jnp.zeros((tile, 128), jnp.float32)
    k = 0
    for ref in row_refs:
        rows_ref[:, k : k + ref.shape[1]] = ref[...]
        for i in range(0, ref.shape[1], 128):
            x = ref[:, i : i + 128].astype(jnp.float32) * degain_ref[:, k + i : k + i + 128]
            squares += x * x
        k += ref.shape[1]
    mean = jnp.sum(squares, axis=1, keepdims=True) / width
    scale_ref[...] = jnp.broadcast_to(lax.rsqrt(mean + EPSILON) * LOG2E, scale_ref.shape)


def assemble(row_blocks, degain):
    rows, width, tile = row_blocks[0].shape[0], degain.shape[1], 256
    by_tile = lambda columns: pl.BlockSpec((tile, columns), lambda i: (i, 0))
    return pl.pallas_call(
        assemble_kernel,
        out_shape=[
            jax.ShapeDtypeStruct((rows, width), jnp.bfloat16),
            jax.ShapeDtypeStruct((rows, 128), jnp.float32),
        ],
        grid=(rows // tile,),
        in_specs=[
            *(by_tile(b.shape[1]) for b in row_blocks),
            pl.BlockSpec(degain.shape, lambda i: (0, 0)),
        ],
        out_specs=[by_tile(width), by_tile(128)],
        compiler_params=pltpu.CompilerParams(vmem_limit_bytes=VMEM_LIMIT),
        cost_estimate=pl.CostEstimate(
            flops=4 * rows * width, bytes_accessed=4 * rows * width, transcendentals=0
        ),
        name="assemble",
    )(*row_blocks, degain)


def vocab_kernel(
    first_ref, rows_ref, scale_s, label_s, w_ref, out_ref,
    rows_s, first_s, second_s, top_s, sum_s, pick_s, sem,
):
    step = pl.program_id(0)
    rows, width = rows_s.shape
    tile, columns = first_s.shape
    n_tiles = rows // tile
    at_tile = lambda t: slice(t * tile, (t + 1) * tile)
    arrivals = [
        pltpu.make_async_copy(rows_ref.at[at_tile(t)], rows_s.at[at_tile(t)], sem.at[t])
        for t in range(n_tiles)
    ]

    @pl.when(step == 0)
    def _():
        for copy in arrivals:
            copy.start()
        top_s[...] = jnp.full_like(top_s, MASKED)
        sum_s[...] = jnp.zeros_like(sum_s)
        pick_s[...] = jnp.zeros_like(pick_s)

    lane = lax.broadcasted_iota(jnp.int32, (1, 128), 1)

    def take(at, product_ref, first_column):
        scale = scale_s[at, :]
        logits = [product_ref[:, c : c + 128] * scale for c in range(0, columns, 128)]
        old = top_s[at, :]
        top = old
        for part in logits:
            top = jnp.maximum(top, part)
        total = sum_s[at, :] * jnp.exp2(old - top)
        pick = pick_s[at, :]
        place = label_s[at, :] - (first_column + lane)
        for c, part in enumerate(logits):
            total += jnp.exp2(part - top)
            pick = jnp.where(place == c * 128, part, pick)
        top_s[at, :] = top
        sum_s[at, :] = total
        pick_s[at, :] = pick

    first_column = first_ref[0] + step * first_ref[1]
    products = (first_s, second_s)
    for t in range(n_tiles):

        @pl.when(step == 0)
        def _():
            arrivals[t].wait()

        product = jnp.dot(rows_s[at_tile(t), :], w_ref[0], preferred_element_type=jnp.float32)
        if t:
            take(at_tile(t - 1), products[(t + 1) % 2], first_column)
        products[t % 2][...] = product
    take(at_tile(n_tiles - 1), products[(n_tiles + 1) % 2], first_column)

    @pl.when(step == pl.num_programs(0) - 1)
    def _():
        top = jnp.max(top_s[...], axis=1, keepdims=True)
        total = jnp.sum(sum_s[...] * jnp.exp2(top_s[...] - top), axis=1, keepdims=True)
        total = top * (1.0 / LOG2E) + jnp.log(total)
        pick = jnp.sum(pick_s[...], axis=1, keepdims=True) * (1.0 / LOG2E)
        both = jnp.where(lane == 0, total, jnp.where(lane == 1, pick, 0.0))
        out_ref[...] = both.T[:8, :]


def vocab_stats(first, rows, scale, row_labels, vocab_all):
    n_rows, width = rows.shape
    n_blocks, _, columns = vocab_all.shape
    tile = 256
    whole = lambda shape: pl.BlockSpec(shape, lambda j, f: (0, 0))
    return pl.pallas_call(
        vocab_kernel,
        out_shape=jax.ShapeDtypeStruct((8, n_rows), jnp.float32),
        grid_spec=pltpu.PrefetchScalarGridSpec(
            num_scalar_prefetch=1,
            grid=(n_blocks,),
            in_specs=[
                pl.BlockSpec(memory_space=pl.ANY),
                whole(scale.shape),
                whole(row_labels.shape),
                pl.BlockSpec((1, width, columns), lambda j, f: (j, 0, 0)),
            ],
            out_specs=whole((8, n_rows)),
            scratch_shapes=[
                pltpu.VMEM((n_rows, width), jnp.bfloat16),
                *(pltpu.VMEM((tile, columns), jnp.float32) for _ in range(2)),
                *(pltpu.VMEM((n_rows, 128), jnp.float32) for _ in range(3)),
                pltpu.SemaphoreType.DMA((n_rows // tile,)),
            ],
        ),
        compiler_params=pltpu.CompilerParams(vmem_limit_bytes=VMEM_LIMIT),
        cost_estimate=pl.CostEstimate(
            flops=2 * n_rows * width * n_blocks * columns,
            bytes_accessed=n_rows * width * 2 + n_blocks * width * columns * 2,
            transcendentals=n_rows * n_blocks * columns,
        ),
        name="vocab_stats",
    )(first, rows, scale, row_labels, vocab_all)


def piece_kernel(row_ref, vocab_ref, piece_ref, sem):
    part = piece_ref.shape[0] // 2
    started = [
        pltpu.make_async_copy(
            vocab_ref.at[pl.ds(pl.multiple_of(row_ref[i] * part, part), part)],
            piece_ref.at[i * part : (i + 1) * part],
            sem.at[i],
        )
        for i in range(2)
    ]
    for copy in started:
        copy.start()
    for copy in started:
        copy.wait()


def vocab_piece(places, w_vocab, part):
    return pl.pallas_call(
        piece_kernel,
        out_shape=jax.ShapeDtypeStruct((2 * part, w_vocab.shape[1]), jnp.bfloat16),
        grid_spec=pltpu.PrefetchScalarGridSpec(
            num_scalar_prefetch=1,
            grid=(),
            in_specs=[pl.BlockSpec(memory_space=pl.ANY)],
            out_specs=pl.BlockSpec(memory_space=pltpu.VMEM),
            scratch_shapes=[pltpu.SemaphoreType.DMA((2,))],
        ),
        compiler_params=pltpu.CompilerParams(vmem_limit_bytes=VMEM_LIMIT),
        cost_estimate=pl.CostEstimate(flops=0, bytes_accessed=2 << 20, transcendentals=0),
        name="vocab_piece",
    )(places, w_vocab)


def split_kernel(w_ref, out_ref):
    part = out_ref.shape[2]
    for i in range(out_ref.shape[0]):
        out_ref[i] = w_ref[:, i * part : (i + 1) * part]


def split_columns(w, n):
    rows, columns = w.shape
    part = columns // n
    return pl.pallas_call(
        split_kernel,
        out_shape=jax.ShapeDtypeStruct((n, rows, part), w.dtype),
        grid=(2,),
        in_specs=[pl.BlockSpec((rows, columns // 2), lambda i: (0, i))],
        out_specs=pl.BlockSpec((n // 2, rows, part), lambda i: (i, 0, 0)),
        cost_estimate=pl.CostEstimate(flops=0, bytes_accessed=4 << 20, transcendentals=0),
        name="split_columns",
    )(w)


def order_kernel(place_ref, in_ref, out_ref, sem):
    n, width, _ = in_ref.shape
    started = [
        pltpu.make_async_copy(
            in_ref.at[place_ref[i]], out_ref.at[i * width : (i + 1) * width], sem.at[i]
        )
        for i in range(n)
    ]
    for copy in started:
        copy.start()
    for copy in started:
        copy.wait()


def in_ring_order(places, blocks):
    n, width, part = blocks.shape
    anywhere = pl.BlockSpec(memory_space=pl.ANY)
    return pl.pallas_call(
        order_kernel,
        out_shape=jax.ShapeDtypeStruct((n * width, part), blocks.dtype),
        grid_spec=pltpu.PrefetchScalarGridSpec(
            num_scalar_prefetch=1,
            grid=(),
            in_specs=[anywhere],
            out_specs=pl.BlockSpec(memory_space=pltpu.VMEM),
            scratch_shapes=[pltpu.SemaphoreType.DMA((n,))],
        ),
        compiler_params=pltpu.CompilerParams(vmem_limit_bytes=VMEM_LIMIT),
        cost_estimate=pl.CostEstimate(flops=0, bytes_accessed=4 << 20, transcendentals=0),
        name="in_ring_order",
    )(places, blocks)


def shards(prompts, target_embed, labels, lengths, attn_gain, w_qkv, w_out, final_gain, w_vocab):
    n_prompt = lax.axis_size("prompt")
    n_dp = lax.axis_size("dp")
    n_model = lax.axis_size(MP)
    prompts_here = prompts.shape[0]
    target_len = target_embed.shape[1]
    model_width = target_embed.shape[2]
    vocab_cols = w_vocab.shape[1]
    heads_width = w_out.shape[0]
    z_index = lax.axis_index("mp_0")
    core = lax.axis_index("mp_1")
    part = model_width // n_model
    places = [((z_index + r) % 4) * 2 + (core + k) % 2 for r in RING for k in range(2)]

    place_ids = jnp.stack(places).astype(jnp.int32)
    x_index = lax.axis_index("prompt")
    turn = jnp.where(x_index == 0, 0, jnp.where(x_index == 1, 3, x_index - 1))
    my_pair = ((z_index + turn) % 4) * 2
    pair = jnp.stack([my_pair + core, my_pair + 1 - core]).astype(jnp.int32)
    piece = vocab_piece(pair, w_vocab, part)
    vocab_all = lax.all_gather(piece, ("dp", "prompt"), axis=0, tiled=True)
    vocab_all = vocab_all.reshape(n_dp, model_width, vocab_cols)
    by_part = split_columns(w_out, n_model)
    out_cols = lax.all_to_all(by_part, MP, split_axis=0, concat_axis=0, tiled=True)

    halves = attention(target_embed, prompts, attn_gain, w_qkv)
    contexts = whole_row(*halves)
    out_cols = in_ring_order(place_ids, out_cols)
    halves = output_part(place_ids[:1], contexts, out_cols, target_embed, final_gain)
    row_blocks = whole_row(*halves)

    degain = 1.0 / jnp.concatenate(
        [lax.dynamic_slice_in_dim(final_gain, p * part, part, 0) for p in places], axis=0
    ).reshape(1, -1)
    row_labels = jnp.tile(labels.reshape(-1, 1), (prompts_here, 128))
    rows, scale = assemble(row_blocks, degain)
    first = jnp.stack([lax.axis_index(MP) * vocab_cols, n_model * vocab_cols]).astype(jnp.int32)
    here = vocab_stats(first, rows, scale, row_labels, vocab_all)[:2]

    every = lax.all_gather(here, MP)
    top_val = jnp.max(every[:, 0], axis=0)
    log_total = top_val + jnp.log(jnp.sum(jnp.exp(every[:, 0] - top_val), axis=0))
    losses = (log_total - jnp.sum(every[:, 1], axis=0)).reshape(prompts_here, 1, target_len)
    valid = jnp.arange(target_len, dtype=jnp.int32)[None, :] < lengths[:, None]
    token_loss = jnp.where(valid[None], losses, 0.0)
    prompt_sums = jnp.sum(token_loss, axis=(1, 2))
    all_prompts = prompts_here * n_prompt
    slot_ids = lax.axis_index("prompt") * prompts_here + jnp.arange(prompts_here, dtype=jnp.int32)
    placed = jnp.sum(
        jnp.where(
            jnp.arange(all_prompts, dtype=jnp.int32)[:, None] == slot_ids[None, :],
            prompt_sums[None, :],
            0.0,
        ),
        axis=1,
    )
    valid_here = jnp.sum(lengths).astype(jnp.float32).reshape(1)
    totals = of_everyone(jnp.concatenate([placed, valid_here]), ("prompt", "dp"))
    prompt_loss = totals[:all_prompts] * float(n_prompt) / totals[all_prompts]
    return (token_loss, prompt_loss)


def solution(mesh):
    finer = Mesh(
        mesh.devices.reshape(mesh.shape["prompt"], mesh.shape["dp"], 4, 2),
        ("prompt", "dp", "mp_0", "mp_1"),
    )
    return jax.shard_map(
        shards,
        mesh=finer,
        in_specs=(
            P("prompt", None, None),
            P("dp", None, None),
            P("dp", None),
            P("dp"),
            P(),
            P(None, None, MP),
            P(MP, None),
            P(),
            P(None, ("dp", "mp_0", "mp_1")),
        ),
        out_specs=(P("prompt", "dp", None), P()),
        check_vma=False,
    )
```

```python
import math

import jax
import jax.numpy as jnp
import numpy as np
from jax import lax
from jax.experimental import pallas as pl
from jax.experimental.pallas import tpu as pltpu
from jax.sharding import Mesh
from jax.sharding import PartitionSpec as P

HD = 128
MP = ("mp_0", "mp_1")
RING = (0, 3, 1, 2)
EPSILON = 1e-05
BASE_THETA = 10000.0
MASKED = -1e30
VMEM_LIMIT = 56 << 20
LOG2E = math.log2(math.e)


def of_everyone(value, axis):
    copies = jnp.broadcast_to(value, (lax.axis_size(axis), *value.shape))
    everything = lax.all_to_all(copies, axis, split_axis=0, concat_axis=0, tiled=True)
    return jnp.sum(everything, axis=0)


def shifted(value, axis, shift):
    n = lax.axis_size(axis)
    return lax.ppermute(value, axis, [(i, (i + shift) % n) for i in range(n)])


def ring_pairs(left, right, axis):
    left_before = shifted(left, axis, 1)
    right_after = shifted(right, axis, -1)
    right_before = shifted(right, axis, 1)
    left_after = shifted(left, axis, -1)
    left_far = shifted(left_before, axis, 1)
    right_far = shifted(right_after, axis, -1)
    return [
        (left, right),
        (left_before, right_before),
        (left_after, right_after),
        (left_far, right_far),
    ]


def whole_row(left, right):
    pairs = ring_pairs(left, right, "mp_0")
    return [b for pair in pairs for b in (*pair, *(shifted(half, "mp_1", 1) for half in pair))]


def rope_tables(number_rows, offset):
    positions = np.arange(offset, offset + number_rows, dtype=np.float32)
    indices_f = np.arange(HD // 2, dtype=np.float32)
    frequency = np.exp(indices_f * np.float32(-2.0 * math.log(BASE_THETA) / HD))
    angles = positions[:, None] * frequency[None, :]
    return jnp.asarray(np.cos(angles)), jnp.asarray(np.sin(angles))


def attention_kernel(
    target_ref, prompt_ref, gain_ref, w_ref, cos_t, sin_t, cos_p, sin_p, left_ref, right_ref,
    acc_t, acc_p, sq_t, sq_p, q_s, k_s, v_s, kp_s, vp_s,
):
    step = pl.program_id(0)
    n_prompts = prompt_ref.shape[0]

    @pl.when(step == 0)
    def _():
        acc_t[...] = jnp.zeros_like(acc_t)
        acc_p[...] = jnp.zeros_like(acc_p)
        sq_t[...] = jnp.zeros_like(sq_t)
        sq_p[...] = jnp.zeros_like(sq_p)

    gain = gain_ref[...]

    def lanes_of_squares(x):
        square = x * x
        return sum(square[:, i : i + 128] for i in range(0, square.shape[1], 128))

    x = target_ref[0].astype(jnp.float32)
    sq_t[...] += lanes_of_squares(x)
    scaled = (x * gain).astype(jnp.bfloat16)
    for c in range(3):
        acc_t[c] += jnp.dot(scaled, w_ref[c], preferred_element_type=jnp.float32)
    for p in range(n_prompts):
        x = prompt_ref[p].astype(jnp.float32)
        sq_p[p] += lanes_of_squares(x)
        scaled = (x * gain).astype(jnp.bfloat16)
        for c in range(2):
            acc_p[p, c] += jnp.dot(scaled, w_ref[c + 1], preferred_element_type=jnp.float32)

    @pl.when(step == pl.num_programs(0) - 1)
    def _():
        width = pl.num_programs(0) * target_ref.shape[2]
        heads = q_s.shape[1] // HD

        def inverse(square):
            return lax.rsqrt(jnp.sum(square, axis=1, keepdims=True) / width + EPSILON)

        def turned(values, cos, sin):
            cos = jnp.concatenate([cos, cos], axis=1)
            sin = jnp.concatenate([-sin, sin], axis=1)
            return values * cos + pltpu.roll(values, HD // 2, 1) * sin

        scale_t = inverse(sq_t[...])
        for h in range(heads):
            at = slice(h * HD, (h + 1) * HD)
            q_s[:, at] = turned(acc_t[0, :, at] * scale_t, cos_t[...], sin_t[...]).astype(jnp.bfloat16)
            k_s[:, at] = turned(acc_t[1, :, at] * scale_t, cos_t[...], sin_t[...]).astype(jnp.bfloat16)
            v_s[:, at] = (acc_t[2, :, at] * scale_t).astype(jnp.bfloat16)
            for p in range(n_prompts):
                scale_p = inverse(sq_p[p])
                kp_s[p, :, at] = turned(
                    acc_p[p, 0, :, at] * scale_p, cos_p[...], sin_p[...]
                ).astype(jnp.bfloat16)
                vp_s[p, :, at] = (acc_p[p, 1, :, at] * scale_p).astype(jnp.bfloat16)
        target_len = q_s.shape[0]
        tile = target_len // 2
        transposed = (((1,), (1,)), ((), ()))
        def one_prompt(p, carry):
            for h in range(heads):
                at = slice(h * HD, (h + 1) * HD)
                for first in range(0, target_len, tile):
                    seen = first + tile
                    q = q_s[first:seen, at]
                    near = lax.dot_general(
                        q, kp_s[p, :, at], transposed, preferred_element_type=jnp.float32
                    ) * HD ** (-0.5)
                    own = lax.dot_general(
                        q, k_s[:seen, at], transposed, preferred_element_type=jnp.float32
                    ) * HD ** (-0.5)
                    row = first + lax.broadcasted_iota(jnp.int32, own.shape, 0)
                    key = lax.broadcasted_iota(jnp.int32, own.shape, 1)
                    own = jnp.where(key <= row, own, MASKED)
                    top = jnp.maximum(
                        jnp.max(near, axis=1, keepdims=True), jnp.max(own, axis=1, keepdims=True)
                    )
                    near = jnp.exp(near - top)
                    own = jnp.exp(own - top)
                    norm = 1.0 / (
                        jnp.sum(near, axis=1, keepdims=True) + jnp.sum(own, axis=1, keepdims=True)
                    )
                    context = jnp.dot(
                        (near * norm).astype(jnp.bfloat16),
                        vp_s[p, :, at],
                        preferred_element_type=jnp.float32,
                    ) + jnp.dot(
                        (own * norm).astype(jnp.bfloat16),
                        v_s[:seen, at],
                        preferred_element_type=jnp.float32,
                    )
                    out_ref = (left_ref, right_ref)[h]
                    rows = pl.ds(pl.multiple_of(p * target_len + first, tile), tile)
                    out_ref[rows, :] = context.astype(jnp.bfloat16)
            return carry

        lax.fori_loop(0, n_prompts, one_prompt, 0)


def attention(target_embed, prompts, attn_gain, w_qkv):
    n_prompts, prompt_len, width = prompts.shape
    target_len = target_embed.shape[1]
    inner = w_qkv.shape[2]
    chunk = 512
    tables = (*rope_tables(target_len, prompt_len), *rope_tables(prompt_len, 0))
    whole = lambda shape: pl.BlockSpec(shape, lambda k: (0,) * len(shape))
    rows = n_prompts * target_len
    return pl.pallas_call(
        attention_kernel,
        out_shape=[jax.ShapeDtypeStruct((rows, inner // 2), jnp.bfloat16)] * 2,
        grid=(width // chunk,),
        in_specs=[
            pl.BlockSpec((1, target_len, chunk), lambda k: (0, 0, k)),
            pl.BlockSpec((n_prompts, prompt_len, chunk), lambda k: (0, 0, k)),
            pl.BlockSpec((1, chunk), lambda k: (0, k)),
            pl.BlockSpec((3, chunk, inner), lambda k: (0, k, 0)),
            *(whole(t.shape) for t in tables),
        ],
        out_specs=[whole((rows, inner // 2))] * 2,
        scratch_shapes=[
            pltpu.VMEM((3, target_len, inner), jnp.float32),
            pltpu.VMEM((n_prompts, 2, prompt_len, inner), jnp.float32),
            pltpu.VMEM((target_len, 128), jnp.float32),
            pltpu.VMEM((n_prompts, prompt_len, 128), jnp.float32),
            *(pltpu.VMEM((target_len, inner), jnp.bfloat16) for _ in range(3)),
            *(pltpu.VMEM((n_prompts, prompt_len, inner), jnp.bfloat16) for _ in range(2)),
        ],
        compiler_params=pltpu.CompilerParams(vmem_limit_bytes=VMEM_LIMIT),
        cost_estimate=pl.CostEstimate(
            flops=8 * 10**9, bytes_accessed=12 * 10**6, transcendentals=2 * 10**6
        ),
        name="attention",
    )(target_embed, prompts, attn_gain.reshape(1, -1), w_qkv, *tables)


def output_kernel(places_ref, *refs):
    *ctx_refs, w_ref, embed_ref, gain_ref, left_ref, right_ref, ctx_s = refs
    at = 0
    for ref in ctx_refs:
        ctx_s[:, at : at + ref.shape[1]] = ref[...]
        at += ref.shape[1]

    total = embed_ref[0].astype(jnp.float32) + jnp.dot(
        ctx_s[...], w_ref[...], preferred_element_type=jnp.float32
    )
    scaled = (total * gain_ref[...]).astype(jnp.bfloat16)
    half = scaled.shape[1] // 2
    left_ref[...] = scaled[:, :half]
    right_ref[...] = scaled[:, half:]


def output_part(place, contexts, out_cols, target_embed, final_gain):
    rows = contexts[0].shape[0]
    inner, part = out_cols.shape
    target_len = target_embed.shape[1]
    tile = target_len // 2
    return pl.pallas_call(
        output_kernel,
        out_shape=[jax.ShapeDtypeStruct((rows, part // 2), jnp.bfloat16)] * 2,
        grid_spec=pltpu.PrefetchScalarGridSpec(
            num_scalar_prefetch=1,
            grid=(rows // tile,),
            in_specs=[
                *(pl.BlockSpec((tile, c.shape[1]), lambda i, at: (i, 0)) for c in contexts),
                pl.BlockSpec(out_cols.shape, lambda i, at: (0, 0)),
                pl.BlockSpec((1, tile, part), lambda i, at: (0, i % 2, at[0])),
                pl.BlockSpec((1, part), lambda i, at: (0, at[0])),
            ],
            out_specs=[pl.BlockSpec((tile, part // 2), lambda i, at: (i, 0))] * 2,
            scratch_shapes=[pltpu.VMEM((tile, inner), jnp.bfloat16)],
        ),
        compiler_params=pltpu.CompilerParams(vmem_limit_bytes=VMEM_LIMIT),
        cost_estimate=pl.CostEstimate(
            flops=2 * 10**9, bytes_accessed=8 * 10**6, transcendentals=0
        ),
        name="output_part",
    )(place, *contexts, out_cols, target_embed, final_gain.reshape(1, -1))


def vocab_kernel(first_ref, *refs, n_rows):
    row_refs = refs[:n_rows]
    degain_ref, label_s, w_ref, out_ref = refs[n_rows : n_rows + 4]
    rows_s, first_s, second_s, top_s, sum_s, pick_s, scale_s = refs[n_rows + 4 :]
    step = pl.program_id(0)
    n_steps = pl.num_programs(0)
    rows, width = rows_s.shape
    tile, columns = first_s.shape
    n_tiles = rows // tile
    at_tile = lambda t: slice(t * tile, (t + 1) * tile)
    lane = lax.broadcasted_iota(jnp.int32, (1, 128), 1)

    @pl.when(step == 0)
    def _():
        squares = jnp.zeros((rows, 128), jnp.float32)
        k = 0
        for ref in row_refs:
            rows_s[:, k : k + ref.shape[1]] = ref[...]
            for i in range(0, ref.shape[1], 128):
                x = ref[:, i : i + 128].astype(jnp.float32) * degain_ref[:, k + i : k + i + 128]
                squares += x * x
            k += ref.shape[1]
        mean = jnp.sum(squares, axis=1, keepdims=True) / width
        scale_s[...] = jnp.broadcast_to(lax.rsqrt(mean + EPSILON) * LOG2E, scale_s.shape)
        top_s[...] = jnp.full_like(top_s, MASKED)
        sum_s[...] = jnp.zeros_like(sum_s)
        pick_s[...] = jnp.zeros_like(pick_s)

    def take(at, product_ref, first_column):
        scale = scale_s[at, :]
        logits = [product_ref[:, c : c + 128] * scale for c in range(0, columns, 128)]
        old = top_s[at, :]
        top = old
        for part in logits:
            top = jnp.maximum(top, part)
        total = sum_s[at, :] * jnp.exp2(old - top)
        pick = pick_s[at, :]
        place = label_s[at, :] - (first_column + lane)
        for c, part in enumerate(logits):
            total += jnp.exp2(part - top)
            pick = jnp.where(place == c * 128, part, pick)
        top_s[at, :] = top
        sum_s[at, :] = total
        pick_s[at, :] = pick

    first_column = first_ref[0] + step * first_ref[1]
    products = (first_s, second_s)
    for t in range(n_tiles):
        product = jnp.dot(rows_s[at_tile(t), :], w_ref[0], preferred_element_type=jnp.float32)
        if t:
            take(at_tile(t - 1), products[(t + 1) % 2], first_column)
        products[t % 2][...] = product
    take(at_tile(n_tiles - 1), products[(n_tiles + 1) % 2], first_column)

    @pl.when(step == n_steps - 1)
    def _():
        top = jnp.max(top_s[...], axis=1, keepdims=True)
        total = jnp.sum(sum_s[...] * jnp.exp2(top_s[...] - top), axis=1, keepdims=True)
        total = top * (1.0 / LOG2E) + jnp.log(total)
        pick = jnp.sum(pick_s[...], axis=1, keepdims=True) * (1.0 / LOG2E)
        both = jnp.where(lane == 0, total, jnp.where(lane == 1, pick, 0.0))
        out_ref[...] = both.T[:8, :]


def vocab_stats(first, row_blocks, degain, row_labels, vocab_all):
    n_rows = row_blocks[0].shape[0]
    n_blocks, width, columns = vocab_all.shape
    tile = 256
    whole = lambda a: pl.BlockSpec(a.shape, lambda j, f: (0, 0), pipeline_mode=pl.Buffered(1))
    kernel = lambda *refs: vocab_kernel(*refs, n_rows=len(row_blocks))
    return pl.pallas_call(
        kernel,
        out_shape=jax.ShapeDtypeStruct((8, n_rows), jnp.float32),
        grid_spec=pltpu.PrefetchScalarGridSpec(
            num_scalar_prefetch=1,
            grid=(n_blocks,),
            in_specs=[
                *(whole(b) for b in row_blocks),
                whole(degain),
                whole(row_labels),
                pl.BlockSpec((1, width, columns), lambda j, f: (j, 0, 0)),
            ],
            out_specs=pl.BlockSpec((8, n_rows), lambda j, f: (0, 0)),
            scratch_shapes=[
                pltpu.VMEM((n_rows, width), jnp.bfloat16),
                *(pltpu.VMEM((tile, columns), jnp.float32) for _ in range(2)),
                *(pltpu.VMEM((n_rows, 128), jnp.float32) for _ in range(4)),
            ],
        ),
        compiler_params=pltpu.CompilerParams(vmem_limit_bytes=VMEM_LIMIT),
        cost_estimate=pl.CostEstimate(
            flops=2 * n_rows * width * n_blocks * columns,
            bytes_accessed=n_rows * width * 2 + n_blocks * width * columns * 2,
            transcendentals=n_rows * n_blocks * columns,
        ),
        name="vocab_stats",
    )(first, *row_blocks, degain, row_labels, vocab_all)


def piece_kernel(row_ref, vocab_ref, piece_ref, sem):
    part = piece_ref.shape[0] // 2
    started = [
        pltpu.make_async_copy(
            vocab_ref.at[pl.ds(pl.multiple_of(row_ref[i] * part, part), part)],
            piece_ref.at[i * part : (i + 1) * part],
            sem.at[i],
        )
        for i in range(2)
    ]
    for copy in started:
        copy.start()
    for copy in started:
        copy.wait()


def vocab_piece(places, w_vocab, part):
    return pl.pallas_call(
        piece_kernel,
        out_shape=jax.ShapeDtypeStruct((2 * part, w_vocab.shape[1]), jnp.bfloat16),
        grid_spec=pltpu.PrefetchScalarGridSpec(
            num_scalar_prefetch=1,
            grid=(),
            in_specs=[pl.BlockSpec(memory_space=pl.ANY)],
            out_specs=pl.BlockSpec(memory_space=pltpu.VMEM),
            scratch_shapes=[pltpu.SemaphoreType.DMA((2,))],
        ),
        compiler_params=pltpu.CompilerParams(vmem_limit_bytes=VMEM_LIMIT),
        cost_estimate=pl.CostEstimate(flops=0, bytes_accessed=2 << 20, transcendentals=0),
        name="vocab_piece",
    )(places, w_vocab)


def split_kernel(w_ref, out_ref):
    part = out_ref.shape[2]
    for i in range(out_ref.shape[0]):
        out_ref[i] = w_ref[:, i * part : (i + 1) * part]


def split_columns(w, n):
    rows, columns = w.shape
    part = columns // n
    return pl.pallas_call(
        split_kernel,
        out_shape=jax.ShapeDtypeStruct((n, rows, part), w.dtype),
        grid=(2,),
        in_specs=[pl.BlockSpec((rows, columns // 2), lambda i: (0, i))],
        out_specs=pl.BlockSpec((n // 2, rows, part), lambda i: (i, 0, 0)),
        cost_estimate=pl.CostEstimate(flops=0, bytes_accessed=4 << 20, transcendentals=0),
        name="split_columns",
    )(w)


def order_kernel(place_ref, in_ref, out_ref, sem):
    n, width, _ = in_ref.shape
    started = [
        pltpu.make_async_copy(
            in_ref.at[place_ref[i]], out_ref.at[i * width : (i + 1) * width], sem.at[i]
        )
        for i in range(n)
    ]
    for copy in started:
        copy.start()
    for copy in started:
        copy.wait()


def in_ring_order(places, blocks):
    n, width, part = blocks.shape
    anywhere = pl.BlockSpec(memory_space=pl.ANY)
    return pl.pallas_call(
        order_kernel,
        out_shape=jax.ShapeDtypeStruct((n * width, part), blocks.dtype),
        grid_spec=pltpu.PrefetchScalarGridSpec(
            num_scalar_prefetch=1,
            grid=(),
            in_specs=[anywhere],
            out_specs=pl.BlockSpec(memory_space=pltpu.VMEM),
            scratch_shapes=[pltpu.SemaphoreType.DMA((n,))],
        ),
        compiler_params=pltpu.CompilerParams(vmem_limit_bytes=VMEM_LIMIT),
        cost_estimate=pl.CostEstimate(flops=0, bytes_accessed=4 << 20, transcendentals=0),
        name="in_ring_order",
    )(places, blocks)


def shards(prompts, target_embed, labels, lengths, attn_gain, w_qkv, w_out, final_gain, w_vocab):
    n_prompt = lax.axis_size("prompt")
    n_dp = lax.axis_size("dp")
    n_model = lax.axis_size(MP)
    prompts_here = prompts.shape[0]
    target_len = target_embed.shape[1]
    model_width = target_embed.shape[2]
    vocab_cols = w_vocab.shape[1]
    heads_width = w_out.shape[0]
    z_index = lax.axis_index("mp_0")
    core = lax.axis_index("mp_1")
    part = model_width // n_model
    places = [((z_index + r) % 4) * 2 + (core + k) % 2 for r in RING for k in range(2)]

    place_ids = jnp.stack(places).astype(jnp.int32)
    x_index = lax.axis_index("prompt")
    turn = jnp.where(x_index == 0, 0, jnp.where(x_index == 1, 3, x_index - 1))
    my_pair = ((z_index + turn) % 4) * 2
    pair = jnp.stack([my_pair + core, my_pair + 1 - core]).astype(jnp.int32)
    piece = vocab_piece(pair, w_vocab, part)
    vocab_all = lax.all_gather(piece, ("dp", "prompt"), axis=0, tiled=True)
    vocab_all = vocab_all.reshape(n_dp, model_width, vocab_cols)
    by_part = split_columns(w_out, n_model)
    out_cols = lax.all_to_all(by_part, MP, split_axis=0, concat_axis=0, tiled=True)

    halves = attention(target_embed, prompts, attn_gain, w_qkv)
    contexts = whole_row(*halves)
    out_cols = in_ring_order(place_ids, out_cols)
    halves = output_part(place_ids[:1], contexts, out_cols, target_embed, final_gain)
    row_blocks = whole_row(*halves)

    degain = 1.0 / jnp.concatenate(
        [lax.dynamic_slice_in_dim(final_gain, p * part, part, 0) for p in places], axis=0
    ).reshape(1, -1)
    row_labels = jnp.tile(labels.reshape(-1, 1), (prompts_here, 128))
    first = jnp.stack([lax.axis_index(MP) * vocab_cols, n_model * vocab_cols]).astype(jnp.int32)
    here = vocab_stats(first, row_blocks, degain, row_labels, vocab_all)[:2]

    every = lax.all_gather(here, MP)
    top_val = jnp.max(every[:, 0], axis=0)
    log_total = top_val + jnp.log(jnp.sum(jnp.exp(every[:, 0] - top_val), axis=0))
    losses = (log_total - jnp.sum(every[:, 1], axis=0)).reshape(prompts_here, 1, target_len)
    valid = jnp.arange(target_len, dtype=jnp.int32)[None, :] < lengths[:, None]
    token_loss = jnp.where(valid[None], losses, 0.0)
    prompt_sums = jnp.sum(token_loss, axis=(1, 2))
    all_prompts = prompts_here * n_prompt
    slot_ids = lax.axis_index("prompt") * prompts_here + jnp.arange(prompts_here, dtype=jnp.int32)
    placed = jnp.sum(
        jnp.where(
            jnp.arange(all_prompts, dtype=jnp.int32)[:, None] == slot_ids[None, :],
            prompt_sums[None, :],
            0.0,
        ),
        axis=1,
    )
    valid_here = jnp.sum(lengths).astype(jnp.float32).reshape(1)
    totals = of_everyone(jnp.concatenate([placed, valid_here]), ("prompt", "dp"))
    prompt_loss = totals[:all_prompts] * float(n_prompt) / totals[all_prompts]
    return (token_loss, prompt_loss)


def solution(mesh):
    finer = Mesh(
        mesh.devices.reshape(mesh.shape["prompt"], mesh.shape["dp"], 4, 2),
        ("prompt", "dp", "mp_0", "mp_1"),
    )
    return jax.shard_map(
        shards,
        mesh=finer,
        in_specs=(
            P("prompt", None, None),
            P("dp", None, None),
            P("dp", None),
            P("dp"),
            P(),
            P(None, None, MP),
            P(MP, None),
            P(),
            P(None, ("dp", "mp_0", "mp_1")),
        ),
        out_specs=(P("prompt", "dp", None), P()),
        check_vma=False,
    )
```

```python
import math

import jax
import jax.numpy as jnp
import numpy as np
from jax import lax
from jax.experimental import pallas as pl
from jax.experimental.pallas import tpu as pltpu
from jax.sharding import Mesh
from jax.sharding import PartitionSpec as P

HD = 128
MP = ("mp_0", "mp_1")
RING = (0, 3, 1, 2)
EPSILON = 1e-05
BASE_THETA = 10000.0
MASKED = -1e30
VMEM_LIMIT = 56 << 20
LOG2E = math.log2(math.e)


def of_everyone(value, axis):
    copies = jnp.broadcast_to(value, (lax.axis_size(axis), *value.shape))
    everything = lax.all_to_all(copies, axis, split_axis=0, concat_axis=0, tiled=True)
    return jnp.sum(everything, axis=0)


def shifted(value, axis, shift):
    n = lax.axis_size(axis)
    return lax.ppermute(value, axis, [(i, (i + shift) % n) for i in range(n)])


def ring_pairs(left, right, axis):
    left_before = shifted(left, axis, 1)
    right_after = shifted(right, axis, -1)
    right_before = shifted(right, axis, 1)
    left_after = shifted(left, axis, -1)
    left_far = shifted(left_before, axis, 1)
    right_far = shifted(right_after, axis, -1)
    return [
        (left, right),
        (left_before, right_before),
        (left_after, right_after),
        (left_far, right_far),
    ]


def whole_row(left, right):
    pairs = ring_pairs(left, right, "mp_0")
    return [b for pair in pairs for b in (*pair, *(shifted(half, "mp_1", 1) for half in pair))]


def rope_tables(number_rows, offset):
    positions = np.arange(offset, offset + number_rows, dtype=np.float32)
    indices_f = np.arange(HD // 2, dtype=np.float32)
    frequency = np.exp(indices_f * np.float32(-2.0 * math.log(BASE_THETA) / HD))
    angles = positions[:, None] * frequency[None, :]
    return jnp.asarray(np.cos(angles)), jnp.asarray(np.sin(angles))


def attention_kernel(
    target_ref, prompt_ref, gain_ref, w_ref, cos_t, sin_t, cos_p, sin_p, left_ref, right_ref,
    acc_t, acc_p, sq_t, sq_p, q_s, k_s, v_s, kp_s, vp_s,
):
    step = pl.program_id(0)
    n_prompts = prompt_ref.shape[0]

    @pl.when(step == 0)
    def _():
        acc_t[...] = jnp.zeros_like(acc_t)
        acc_p[...] = jnp.zeros_like(acc_p)
        sq_t[...] = jnp.zeros_like(sq_t)
        sq_p[...] = jnp.zeros_like(sq_p)

    gain = gain_ref[...]

    def lanes_of_squares(x):
        square = x * x
        return sum(square[:, i : i + 128] for i in range(0, square.shape[1], 128))

    x = target_ref[0].astype(jnp.float32)
    sq_t[...] += lanes_of_squares(x)
    scaled = (x * gain).astype(jnp.bfloat16)
    for c in range(3):
        acc_t[c] += jnp.dot(scaled, w_ref[c], preferred_element_type=jnp.float32)
    for p in range(n_prompts):
        x = prompt_ref[p].astype(jnp.float32)
        sq_p[p] += lanes_of_squares(x)
        scaled = (x * gain).astype(jnp.bfloat16)
        for c in range(2):
            acc_p[p, c] += jnp.dot(scaled, w_ref[c + 1], preferred_element_type=jnp.float32)

    @pl.when(step == pl.num_programs(0) - 1)
    def _():
        width = pl.num_programs(0) * target_ref.shape[2]
        heads = q_s.shape[1] // HD

        def inverse(square):
            return lax.rsqrt(jnp.sum(square, axis=1, keepdims=True) / width + EPSILON)

        def turned(values, cos, sin):
            cos = jnp.concatenate([cos, cos], axis=1)
            sin = jnp.concatenate([-sin, sin], axis=1)
            return values * cos + pltpu.roll(values, HD // 2, 1) * sin

        scale_t = inverse(sq_t[...])
        for h in range(heads):
            at = slice(h * HD, (h + 1) * HD)
            q_s[:, at] = turned(acc_t[0, :, at] * scale_t, cos_t[...], sin_t[...]).astype(jnp.bfloat16)
            k_s[:, at] = turned(acc_t[1, :, at] * scale_t, cos_t[...], sin_t[...]).astype(jnp.bfloat16)
            v_s[:, at] = (acc_t[2, :, at] * scale_t).astype(jnp.bfloat16)
            for p in range(n_prompts):
                scale_p = inverse(sq_p[p])
                kp_s[p, :, at] = turned(
                    acc_p[p, 0, :, at] * scale_p, cos_p[...], sin_p[...]
                ).astype(jnp.bfloat16)
                vp_s[p, :, at] = (acc_p[p, 1, :, at] * scale_p).astype(jnp.bfloat16)
        target_len = q_s.shape[0]
        tile = target_len // 2
        transposed = (((1,), (1,)), ((), ()))
        def one_prompt(p, carry):
            for h in range(heads):
                at = slice(h * HD, (h + 1) * HD)
                for first in range(0, target_len, tile):
                    seen = first + tile
                    q = q_s[first:seen, at]
                    near = lax.dot_general(
                        q, kp_s[p, :, at], transposed, preferred_element_type=jnp.float32
                    ) * HD ** (-0.5)
                    own = lax.dot_general(
                        q, k_s[:seen, at], transposed, preferred_element_type=jnp.float32
                    ) * HD ** (-0.5)
                    row = first + lax.broadcasted_iota(jnp.int32, own.shape, 0)
                    key = lax.broadcasted_iota(jnp.int32, own.shape, 1)
                    own = jnp.where(key <= row, own, MASKED)
                    top = jnp.maximum(
                        jnp.max(near, axis=1, keepdims=True), jnp.max(own, axis=1, keepdims=True)
                    )
                    near = jnp.exp(near - top)
                    own = jnp.exp(own - top)
                    norm = 1.0 / (
                        jnp.sum(near, axis=1, keepdims=True) + jnp.sum(own, axis=1, keepdims=True)
                    )
                    context = jnp.dot(
                        (near * norm).astype(jnp.bfloat16),
                        vp_s[p, :, at],
                        preferred_element_type=jnp.float32,
                    ) + jnp.dot(
                        (own * norm).astype(jnp.bfloat16),
                        v_s[:seen, at],
                        preferred_element_type=jnp.float32,
                    )
                    out_ref = (left_ref, right_ref)[h]
                    rows = pl.ds(pl.multiple_of(p * target_len + first, tile), tile)
                    out_ref[rows, :] = context.astype(jnp.bfloat16)
            return carry

        lax.fori_loop(0, n_prompts, one_prompt, 0)


def attention(target_embed, prompts, attn_gain, w_qkv):
    n_prompts, prompt_len, width = prompts.shape
    target_len = target_embed.shape[1]
    inner = w_qkv.shape[2]
    chunk = 1024
    tables = (*rope_tables(target_len, prompt_len), *rope_tables(prompt_len, 0))
    whole = lambda shape: pl.BlockSpec(shape, lambda k: (0,) * len(shape))
    rows = n_prompts * target_len
    return pl.pallas_call(
        attention_kernel,
        out_shape=[jax.ShapeDtypeStruct((rows, inner // 2), jnp.bfloat16)] * 2,
        grid=(width // chunk,),
        in_specs=[
            pl.BlockSpec((1, target_len, chunk), lambda k: (0, 0, k)),
            pl.BlockSpec((n_prompts, prompt_len, chunk), lambda k: (0, 0, k)),
            pl.BlockSpec((1, chunk), lambda k: (0, k)),
            pl.BlockSpec((3, chunk, inner), lambda k: (0, k, 0)),
            *(whole(t.shape) for t in tables),
        ],
        out_specs=[whole((rows, inner // 2))] * 2,
        scratch_shapes=[
            pltpu.VMEM((3, target_len, inner), jnp.float32),
            pltpu.VMEM((n_prompts, 2, prompt_len, inner), jnp.float32),
            pltpu.VMEM((target_len, 128), jnp.float32),
            pltpu.VMEM((n_prompts, prompt_len, 128), jnp.float32),
            *(pltpu.VMEM((target_len, inner), jnp.bfloat16) for _ in range(3)),
            *(pltpu.VMEM((n_prompts, prompt_len, inner), jnp.bfloat16) for _ in range(2)),
        ],
        compiler_params=pltpu.CompilerParams(vmem_limit_bytes=VMEM_LIMIT),
        cost_estimate=pl.CostEstimate(
            flops=8 * 10**9, bytes_accessed=12 * 10**6, transcendentals=2 * 10**6
        ),
        name="attention",
    )(target_embed, prompts, attn_gain.reshape(1, -1), w_qkv, *tables)


def output_kernel(places_ref, *refs):
    *ctx_refs, w_ref, embed_ref, gain_ref, left_ref, right_ref = refs
    total = embed_ref[0].astype(jnp.float32)
    for group in range(w_ref.shape[0]):
        both = jnp.concatenate([ref[...] for ref in ctx_refs[2 * group : 2 * group + 2]], axis=1)
        total += jnp.dot(both, w_ref[places_ref[group]], preferred_element_type=jnp.float32)
    scaled = (total * gain_ref[...]).astype(jnp.bfloat16)
    half = scaled.shape[1] // 2
    left_ref[...] = scaled[:, :half]
    right_ref[...] = scaled[:, half:]


def output_part(places, contexts, out_cols, target_embed, final_gain):
    rows = contexts[0].shape[0]
    part = out_cols.shape[2]
    target_len = target_embed.shape[1]
    tile = target_len
    return pl.pallas_call(
        output_kernel,
        out_shape=[jax.ShapeDtypeStruct((rows, part // 2), jnp.bfloat16)] * 2,
        grid_spec=pltpu.PrefetchScalarGridSpec(
            num_scalar_prefetch=1,
            grid=(rows // tile,),
            in_specs=[
                *(pl.BlockSpec((tile, c.shape[1]), lambda i, at: (i, 0)) for c in contexts),
                pl.BlockSpec(out_cols.shape, lambda i, at: (0, 0, 0)),
                pl.BlockSpec((1, tile, part), lambda i, at: (0, 0, at[0])),
                pl.BlockSpec((1, part), lambda i, at: (0, at[0])),
            ],
            out_specs=[pl.BlockSpec((tile, part // 2), lambda i, at: (i, 0))] * 2,
        ),
        compiler_params=pltpu.CompilerParams(vmem_limit_bytes=VMEM_LIMIT),
        cost_estimate=pl.CostEstimate(
            flops=2 * 10**9, bytes_accessed=8 * 10**6, transcendentals=0
        ),
        name="output_part",
    )(places, *contexts, out_cols, target_embed, final_gain.reshape(1, -1))


def assemble_kernel(*refs):
    *row_refs, degain_ref, rows_ref, scale_ref = refs
    tile, width = rows_ref.shape
    squares = jnp.zeros((tile, 128), jnp.float32)
    k = 0
    for ref in row_refs:
        rows_ref[:, k : k + ref.shape[1]] = ref[...]
        for i in range(0, ref.shape[1], 128):
            x = ref[:, i : i + 128].astype(jnp.float32) * degain_ref[:, k + i : k + i + 128]
            squares += x * x
        k += ref.shape[1]
    mean = jnp.sum(squares, axis=1, keepdims=True) / width
    scale_ref[...] = jnp.broadcast_to(lax.rsqrt(mean + EPSILON) * LOG2E, scale_ref.shape)


def assemble(row_blocks, degain):
    rows, width, tile = row_blocks[0].shape[0], degain.shape[1], 256
    by_tile = lambda columns: pl.BlockSpec((tile, columns), lambda i: (i, 0))
    return pl.pallas_call(
        assemble_kernel,
        out_shape=[
            jax.ShapeDtypeStruct((rows, width), jnp.bfloat16),
            jax.ShapeDtypeStruct((rows, 128), jnp.float32),
        ],
        grid=(rows // tile,),
        in_specs=[
            *(by_tile(b.shape[1]) for b in row_blocks),
            pl.BlockSpec(degain.shape, lambda i: (0, 0)),
        ],
        out_specs=[by_tile(width), by_tile(128)],
        compiler_params=pltpu.CompilerParams(vmem_limit_bytes=VMEM_LIMIT),
        cost_estimate=pl.CostEstimate(
            flops=4 * rows * width, bytes_accessed=4 * rows * width, transcendentals=0
        ),
        name="assemble",
    )(*row_blocks, degain)


def vocab_kernel(
    first_ref, rows_s, scale_s, label_ref, w_ref, out_ref,
    first_s, second_s, top_s, sum_s, pick_s, label_s,
):
    step = pl.program_id(0)
    rows = rows_s.shape[0]
    tile, columns = first_s.shape
    n_tiles = rows // tile
    at_tile = lambda t: slice(t * tile, (t + 1) * tile)
    lane = lax.broadcasted_iota(jnp.int32, (1, 128), 1)

    @pl.when(step == 0)
    def _():
        label_s[...] = jnp.broadcast_to(label_ref[...], label_s.shape)
        top_s[...] = jnp.full_like(top_s, MASKED)
        sum_s[...] = jnp.zeros_like(sum_s)
        pick_s[...] = jnp.zeros_like(pick_s)

    def take(at, product_ref, first_column):
        scale = scale_s[at, :]
        logits = [product_ref[:, c : c + 128] * scale for c in range(0, columns, 128)]
        old = top_s[at, :]
        top = old
        for part in logits:
            top = jnp.maximum(top, part)
        total = sum_s[at, :] * jnp.exp2(old - top)
        pick = pick_s[at, :]
        place = label_s[at, :] - (first_column + lane)
        for c, part in enumerate(logits):
            total += jnp.exp2(part - top)
            pick = jnp.where(place == c * 128, part, pick)
        top_s[at, :] = top
        sum_s[at, :] = total
        pick_s[at, :] = pick

    first_column = first_ref[0] + step * first_ref[1]
    products = (first_s, second_s)
    for t in range(n_tiles):
        product = jnp.dot(rows_s[at_tile(t), :], w_ref[0], preferred_element_type=jnp.float32)
        if t:
            take(at_tile(t - 1), products[(t + 1) % 2], first_column)
        products[t % 2][...] = product
    take(at_tile(n_tiles - 1), products[(n_tiles + 1) % 2], first_column)

    @pl.when(step == pl.num_programs(0) - 1)
    def _():
        top = jnp.max(top_s[...], axis=1, keepdims=True)
        total = jnp.sum(sum_s[...] * jnp.exp2(top_s[...] - top), axis=1, keepdims=True)
        total = top * (1.0 / LOG2E) + jnp.log(total)
        pick = jnp.sum(pick_s[...], axis=1, keepdims=True) * (1.0 / LOG2E)
        both = jnp.where(lane == 0, total, jnp.where(lane == 1, pick, 0.0))
        out_ref[...] = both.T[:2, :]


def vocab_stats(first, rows, scale, row_labels, vocab_all):
    n_rows = rows.shape[0]
    n_blocks, width, columns = vocab_all.shape
    tile = 256
    whole = lambda a: pl.BlockSpec(a.shape, lambda j, f: (0, 0), pipeline_mode=pl.Buffered(1))
    return pl.pallas_call(
        vocab_kernel,
        out_shape=jax.ShapeDtypeStruct((2, n_rows), jnp.float32),
        grid_spec=pltpu.PrefetchScalarGridSpec(
            num_scalar_prefetch=1,
            grid=(n_blocks,),
            in_specs=[
                whole(rows),
                whole(scale),
                whole(row_labels),
                pl.BlockSpec((1, width, columns), lambda j, f: (j, 0, 0)),
            ],
            out_specs=pl.BlockSpec((2, n_rows), lambda j, f: (0, 0)),
            scratch_shapes=[
                *(pltpu.VMEM((tile, columns), jnp.float32) for _ in range(2)),
                *(pltpu.VMEM((n_rows, 128), jnp.float32) for _ in range(3)),
                pltpu.VMEM((n_rows, 128), jnp.int32),
            ],
        ),
        compiler_params=pltpu.CompilerParams(vmem_limit_bytes=VMEM_LIMIT),
        cost_estimate=pl.CostEstimate(
            flops=2 * n_rows * width * n_blocks * columns,
            bytes_accessed=n_rows * width * 2 + n_blocks * width * columns * 2,
            transcendentals=n_rows * n_blocks * columns,
        ),
        name="vocab_stats",
    )(first, rows, scale, row_labels, vocab_all)


def piece_kernel(row_ref, vocab_ref, piece_ref, sem):
    part = piece_ref.shape[0] // 2
    started = [
        pltpu.make_async_copy(
            vocab_ref.at[pl.ds(pl.multiple_of(row_ref[i] * part, part), part)],
            piece_ref.at[i * part : (i + 1) * part],
            sem.at[i],
        )
        for i in range(2)
    ]
    for copy in started:
        copy.start()
    for copy in started:
        copy.wait()


def vocab_piece(places, w_vocab, part):
    return pl.pallas_call(
        piece_kernel,
        out_shape=jax.ShapeDtypeStruct((2 * part, w_vocab.shape[1]), jnp.bfloat16),
        grid_spec=pltpu.PrefetchScalarGridSpec(
            num_scalar_prefetch=1,
            grid=(),
            in_specs=[pl.BlockSpec(memory_space=pl.ANY)],
            out_specs=pl.BlockSpec(memory_space=pltpu.VMEM),
            scratch_shapes=[pltpu.SemaphoreType.DMA((2,))],
        ),
        compiler_params=pltpu.CompilerParams(vmem_limit_bytes=VMEM_LIMIT),
        cost_estimate=pl.CostEstimate(flops=0, bytes_accessed=2 << 20, transcendentals=0),
        name="vocab_piece",
    )(places, w_vocab)


def split_kernel(w_ref, out_ref):
    part = out_ref.shape[2]
    for i in range(out_ref.shape[0]):
        out_ref[i] = w_ref[:, i * part : (i + 1) * part]


def split_columns(w, n):
    rows, columns = w.shape
    part = columns // n
    return pl.pallas_call(
        split_kernel,
        out_shape=jax.ShapeDtypeStruct((n, rows, part), w.dtype),
        grid=(2,),
        in_specs=[pl.BlockSpec((rows, columns // 2), lambda i: (0, i))],
        out_specs=pl.BlockSpec((n // 2, rows, part), lambda i: (i, 0, 0)),
        cost_estimate=pl.CostEstimate(flops=0, bytes_accessed=4 << 20, transcendentals=0),
        name="split_columns",
    )(w)


def shards(prompts, target_embed, labels, lengths, attn_gain, w_qkv, w_out, final_gain, w_vocab):
    n_prompt = lax.axis_size("prompt")
    n_dp = lax.axis_size("dp")
    n_model = lax.axis_size(MP)
    prompts_here = prompts.shape[0]
    target_len = target_embed.shape[1]
    model_width = target_embed.shape[2]
    vocab_cols = w_vocab.shape[1]
    heads_width = w_out.shape[0]
    z_index = lax.axis_index("mp_0")
    core = lax.axis_index("mp_1")
    part = model_width // n_model
    places = [((z_index + r) % 4) * 2 + (core + k) % 2 for r in RING for k in range(2)]

    place_ids = jnp.stack(places).astype(jnp.int32)
    x_index = lax.axis_index("prompt")
    turn = jnp.where(x_index == 0, 0, jnp.where(x_index == 1, 3, x_index - 1))
    my_pair = ((z_index + turn) % 4) * 2
    pair = jnp.stack([my_pair + core, my_pair + 1 - core]).astype(jnp.int32)
    piece = vocab_piece(pair, w_vocab, part)
    vocab_all = lax.all_gather(piece, ("dp", "prompt"), axis=0, tiled=True)
    vocab_all = vocab_all.reshape(n_dp, model_width, vocab_cols)
    by_part = split_columns(w_out, n_model)
    out_cols = lax.all_to_all(by_part, MP, split_axis=0, concat_axis=0, tiled=True)

    halves = attention(target_embed, prompts, attn_gain, w_qkv)
    contexts = whole_row(*halves)
    halves = output_part(place_ids, contexts, out_cols, target_embed, final_gain)
    row_blocks = whole_row(*halves)

    degain = 1.0 / jnp.concatenate(
        [lax.dynamic_slice_in_dim(final_gain, p * part, part, 0) for p in places], axis=0
    ).reshape(1, -1)
    row_labels = jnp.tile(labels.reshape(-1, 1), (prompts_here, 1))
    rows, scale = assemble(row_blocks, degain)
    first = jnp.stack([lax.axis_index(MP) * vocab_cols, n_model * vocab_cols]).astype(jnp.int32)
    here = vocab_stats(first, rows, scale, row_labels, vocab_all)

    every = lax.all_gather(here, MP)
    top_val = jnp.max(every[:, 0], axis=0)
    log_total = top_val + jnp.log(jnp.sum(jnp.exp(every[:, 0] - top_val), axis=0))
    losses = (log_total - jnp.sum(every[:, 1], axis=0)).reshape(prompts_here, 1, target_len)
    valid = jnp.arange(target_len, dtype=jnp.int32)[None, :] < lengths[:, None]
    token_loss = jnp.where(valid[None], losses, 0.0)
    prompt_sums = jnp.sum(token_loss, axis=(1, 2))
    all_prompts = prompts_here * n_prompt
    slot_ids = lax.axis_index("prompt") * prompts_here + jnp.arange(prompts_here, dtype=jnp.int32)
    placed = jnp.sum(
        jnp.where(
            jnp.arange(all_prompts, dtype=jnp.int32)[:, None] == slot_ids[None, :],
            prompt_sums[None, :],
            0.0,
        ),
        axis=1,
    )
    valid_here = jnp.sum(lengths).astype(jnp.float32).reshape(1)
    totals = of_everyone(jnp.concatenate([placed, valid_here]), ("prompt", "dp"))
    prompt_loss = totals[:all_prompts] * float(n_prompt) / totals[all_prompts]
    return (token_loss, prompt_loss)


def solution(mesh):
    finer = Mesh(
        mesh.devices.reshape(mesh.shape["prompt"], mesh.shape["dp"], 4, 2),
        ("prompt", "dp", "mp_0", "mp_1"),
    )
    return jax.shard_map(
        shards,
        mesh=finer,
        in_specs=(
            P("prompt", None, None),
            P("dp", None, None),
            P("dp", None),
            P("dp"),
            P(),
            P(None, None, MP),
            P(MP, None),
            P(),
            P(None, ("dp", "mp_0", "mp_1")),
        ),
        out_specs=(P("prompt", "dp", None), P()),
        check_vma=False,
    )
```

```python
import math

import jax
import jax.numpy as jnp
import numpy as np
from jax import lax
from jax.experimental import pallas as pl
from jax.experimental.pallas import tpu as pltpu
from jax.sharding import Mesh
from jax.sharding import PartitionSpec as P

HD = 128
MP = ("mp_0", "mp_1")
RING = (0, 3, 1, 2)
EPSILON = 1e-05
BASE_THETA = 10000.0
MASKED = -1e30
VMEM_LIMIT = 56 << 20
LOG2E = math.log2(math.e)


def of_each(value, axis):
    copies = jnp.broadcast_to(value, (lax.axis_size(axis), *value.shape))
    return lax.all_to_all(copies, axis, split_axis=0, concat_axis=0, tiled=True)


def shifted(value, axis, shift):
    n = lax.axis_size(axis)
    return lax.ppermute(value, axis, [(i, (i + shift) % n) for i in range(n)])


def ring_pairs(left, right, axis):
    left_before = shifted(left, axis, 1)
    right_after = shifted(right, axis, -1)
    right_before = shifted(right, axis, 1)
    left_after = shifted(left, axis, -1)
    left_far = shifted(left_before, axis, 1)
    right_far = shifted(right_after, axis, -1)
    return [
        (left, right),
        (left_before, right_before),
        (left_after, right_after),
        (left_far, right_far),
    ]


def whole_row(left, right):
    pairs = ring_pairs(left, right, "mp_0")
    return [b for pair in pairs for b in (*pair, *(shifted(half, "mp_1", 1) for half in pair))]


def rope_tables(number_rows, offset):
    positions = np.arange(offset, offset + number_rows, dtype=np.float32)
    indices_f = np.arange(HD // 2, dtype=np.float32)
    frequency = np.exp(indices_f * np.float32(-2.0 * math.log(BASE_THETA) / HD))
    angles = positions[:, None] * frequency[None, :]
    return jnp.asarray(np.cos(angles)), jnp.asarray(np.sin(angles))


def attention_kernel(
    target_ref, prompt_ref, gain_ref, w_ref, cos_t, sin_t, cos_p, sin_p, left_ref, right_ref,
    acc_t, acc_p, sq_t, sq_p, q_s, k_s, v_s, kp_s, vp_s,
):
    step = pl.program_id(0)
    n_prompts = prompt_ref.shape[0]

    @pl.when(step == 0)
    def _():
        acc_t[...] = jnp.zeros_like(acc_t)
        acc_p[...] = jnp.zeros_like(acc_p)
        sq_t[...] = jnp.zeros_like(sq_t)
        sq_p[...] = jnp.zeros_like(sq_p)

    gain = gain_ref[...]

    def lanes_of_squares(x):
        square = x * x
        return sum(square[:, i : i + 128] for i in range(0, square.shape[1], 128))

    x = target_ref[0].astype(jnp.float32)
    sq_t[...] += lanes_of_squares(x)
    scaled = (x * gain).astype(jnp.bfloat16)
    for c in range(3):
        acc_t[c] += jnp.dot(scaled, w_ref[c], preferred_element_type=jnp.float32)
    for p in range(n_prompts):
        x = prompt_ref[p].astype(jnp.float32)
        sq_p[p] += lanes_of_squares(x)
        scaled = (x * gain).astype(jnp.bfloat16)
        for c in range(2):
            acc_p[p, c] += jnp.dot(scaled, w_ref[c + 1], preferred_element_type=jnp.float32)

    @pl.when(step == pl.num_programs(0) - 1)
    def _():
        width = pl.num_programs(0) * target_ref.shape[2]
        heads = q_s.shape[1] // HD

        def inverse(square):
            return lax.rsqrt(jnp.sum(square, axis=1, keepdims=True) / width + EPSILON)

        def turned(values, cos, sin):
            cos = jnp.concatenate([cos, cos], axis=1)
            sin = jnp.concatenate([-sin, sin], axis=1)
            return values * cos + pltpu.roll(values, HD // 2, 1) * sin

        scale_t = inverse(sq_t[...])
        for h in range(heads):
            at = slice(h * HD, (h + 1) * HD)
            q_s[:, at] = turned(acc_t[0, :, at] * scale_t, cos_t[...], sin_t[...]).astype(jnp.bfloat16)
            k_s[:, at] = turned(acc_t[1, :, at] * scale_t, cos_t[...], sin_t[...]).astype(jnp.bfloat16)
            v_s[:, at] = (acc_t[2, :, at] * scale_t).astype(jnp.bfloat16)
            for p in range(n_prompts):
                scale_p = inverse(sq_p[p])
                kp_s[p, :, at] = turned(
                    acc_p[p, 0, :, at] * scale_p, cos_p[...], sin_p[...]
                ).astype(jnp.bfloat16)
                vp_s[p, :, at] = (acc_p[p, 1, :, at] * scale_p).astype(jnp.bfloat16)
        target_len = q_s.shape[0]
        tile = target_len // 2
        transposed = (((1,), (1,)), ((), ()))
        def one_prompt(p, carry):
            for h in range(heads):
                at = slice(h * HD, (h + 1) * HD)
                for first in range(0, target_len, tile):
                    seen = first + tile
                    q = q_s[first:seen, at]
                    near = lax.dot_general(
                        q, kp_s[p, :, at], transposed, preferred_element_type=jnp.float32
                    ) * HD ** (-0.5)
                    own = lax.dot_general(
                        q, k_s[:seen, at], transposed, preferred_element_type=jnp.float32
                    ) * HD ** (-0.5)
                    row = first + lax.broadcasted_iota(jnp.int32, own.shape, 0)
                    key = lax.broadcasted_iota(jnp.int32, own.shape, 1)
                    own = jnp.where(key <= row, own, MASKED)
                    top = jnp.maximum(
                        jnp.max(near, axis=1, keepdims=True), jnp.max(own, axis=1, keepdims=True)
                    )
                    near = jnp.exp(near - top)
                    own = jnp.exp(own - top)
                    norm = 1.0 / (
                        jnp.sum(near, axis=1, keepdims=True) + jnp.sum(own, axis=1, keepdims=True)
                    )
                    context = jnp.dot(
                        (near * norm).astype(jnp.bfloat16),
                        vp_s[p, :, at],
                        preferred_element_type=jnp.float32,
                    ) + jnp.dot(
                        (own * norm).astype(jnp.bfloat16),
                        v_s[:seen, at],
                        preferred_element_type=jnp.float32,
                    )
                    out_ref = (left_ref, right_ref)[h]
                    rows = pl.ds(pl.multiple_of(p * target_len + first, tile), tile)
                    out_ref[rows, :] = context.astype(jnp.bfloat16)
            return carry

        lax.fori_loop(0, n_prompts, one_prompt, 0)


def attention(target_embed, prompts, attn_gain, w_qkv):
    n_prompts, prompt_len, width = prompts.shape
    target_len = target_embed.shape[1]
    inner = w_qkv.shape[2]
    chunk = 1024
    tables = (*rope_tables(target_len, prompt_len), *rope_tables(prompt_len, 0))
    whole = lambda shape: pl.BlockSpec(shape, lambda k: (0,) * len(shape))
    rows = n_prompts * target_len
    return pl.pallas_call(
        attention_kernel,
        out_shape=[jax.ShapeDtypeStruct((rows, inner // 2), jnp.bfloat16)] * 2,
        grid=(width // chunk,),
        in_specs=[
            pl.BlockSpec((1, target_len, chunk), lambda k: (0, 0, k)),
            pl.BlockSpec((n_prompts, prompt_len, chunk), lambda k: (0, 0, k)),
            pl.BlockSpec((1, chunk), lambda k: (0, k)),
            pl.BlockSpec((3, chunk, inner), lambda k: (0, k, 0)),
            *(whole(t.shape) for t in tables),
        ],
        out_specs=[whole((rows, inner // 2))] * 2,
        scratch_shapes=[
            pltpu.VMEM((3, target_len, inner), jnp.float32),
            pltpu.VMEM((n_prompts, 2, prompt_len, inner), jnp.float32),
            pltpu.VMEM((target_len, 128), jnp.float32),
            pltpu.VMEM((n_prompts, prompt_len, 128), jnp.float32),
            *(pltpu.VMEM((target_len, inner), jnp.bfloat16) for _ in range(3)),
            *(pltpu.VMEM((n_prompts, prompt_len, inner), jnp.bfloat16) for _ in range(2)),
        ],
        compiler_params=pltpu.CompilerParams(vmem_limit_bytes=VMEM_LIMIT),
        cost_estimate=pl.CostEstimate(
            flops=8 * 10**9, bytes_accessed=12 * 10**6, transcendentals=2 * 10**6
        ),
        name="attention",
    )(target_embed, prompts, attn_gain.reshape(1, -1), w_qkv, *tables)


def output_kernel(places_ref, *refs):
    *ctx_refs, w_ref, embed_ref, gain_ref, left_ref, right_ref = refs
    total = embed_ref[0].astype(jnp.float32)
    for group in range(w_ref.shape[0]):
        both = jnp.concatenate([ref[...] for ref in ctx_refs[2 * group : 2 * group + 2]], axis=1)
        total += jnp.dot(both, w_ref[places_ref[group]], preferred_element_type=jnp.float32)
    scaled = (total * gain_ref[...]).astype(jnp.bfloat16)
    half = scaled.shape[1] // 2
    left_ref[...] = scaled[:, :half]
    right_ref[...] = scaled[:, half:]


def output_part(places, contexts, out_cols, target_embed, final_gain):
    rows = contexts[0].shape[0]
    part = out_cols.shape[2]
    target_len = target_embed.shape[1]
    tile = target_len
    return pl.pallas_call(
        output_kernel,
        out_shape=[jax.ShapeDtypeStruct((rows, part // 2), jnp.bfloat16)] * 2,
        grid_spec=pltpu.PrefetchScalarGridSpec(
            num_scalar_prefetch=1,
            grid=(rows // tile,),
            in_specs=[
                *(pl.BlockSpec((tile, c.shape[1]), lambda i, at: (i, 0)) for c in contexts),
                pl.BlockSpec(out_cols.shape, lambda i, at: (0, 0, 0)),
                pl.BlockSpec((1, tile, part), lambda i, at: (0, 0, at[0])),
                pl.BlockSpec((1, part), lambda i, at: (0, at[0])),
            ],
            out_specs=[pl.BlockSpec((tile, part // 2), lambda i, at: (i, 0))] * 2,
        ),
        compiler_params=pltpu.CompilerParams(vmem_limit_bytes=VMEM_LIMIT),
        cost_estimate=pl.CostEstimate(
            flops=2 * 10**9, bytes_accessed=8 * 10**6, transcendentals=0
        ),
        name="output_part",
    )(places, *contexts, out_cols, target_embed, final_gain.reshape(1, -1))


def vocab_kernel(first_ref, *refs, n_rows):
    row_refs = refs[:n_rows]
    degain_ref, label_ref, w_ref, out_ref = refs[n_rows : n_rows + 4]
    rows_s, first_s, second_s, top_s, sum_s, pick_s, scale_s, label_s = refs[n_rows + 4 :]
    step = pl.program_id(0)
    n_steps = pl.num_programs(0)
    rows, width = rows_s.shape
    tile, columns = first_s.shape
    n_tiles = rows // tile
    at_tile = lambda t: slice(t * tile, (t + 1) * tile)
    lane = lax.broadcasted_iota(jnp.int32, (1, 128), 1)

    @pl.when(step == 0)
    def _():
        squares = jnp.zeros((rows, 128), jnp.float32)
        k = 0
        for ref in row_refs:
            rows_s[:, k : k + ref.shape[1]] = ref[...]
            for i in range(0, ref.shape[1], 128):
                x = ref[:, i : i + 128].astype(jnp.float32) * degain_ref[:, k + i : k + i + 128]
                squares += x * x
            k += ref.shape[1]
        mean = jnp.sum(squares, axis=1, keepdims=True) / width
        scale_s[...] = jnp.broadcast_to(lax.rsqrt(mean + EPSILON) * LOG2E, scale_s.shape)
        label_s[...] = jnp.broadcast_to(label_ref[...], label_s.shape)
        top_s[...] = jnp.full_like(top_s, MASKED)
        sum_s[...] = jnp.zeros_like(sum_s)
        pick_s[...] = jnp.zeros_like(pick_s)

    def take(at, product_ref, first_column):
        scale = scale_s[at, :]
        logits = [product_ref[:, c : c + 128] * scale for c in range(0, columns, 128)]
        old = top_s[at, :]
        top = old
        for part in logits:
            top = jnp.maximum(top, part)
        total = sum_s[at, :] * jnp.exp2(old - top)
        pick = pick_s[at, :]
        place = label_s[at, :] - (first_column + lane)
        for c, part in enumerate(logits):
            total += jnp.exp2(part - top)
            pick = jnp.where(place == c * 128, part, pick)
        top_s[at, :] = top
        sum_s[at, :] = total
        pick_s[at, :] = pick

    first_column = first_ref[0] + step * first_ref[1]
    products = (first_s, second_s)
    for t in range(n_tiles):
        product = jnp.dot(rows_s[at_tile(t), :], w_ref[0], preferred_element_type=jnp.float32)
        if t:
            take(at_tile(t - 1), products[(t + 1) % 2], first_column)
        products[t % 2][...] = product
    take(at_tile(n_tiles - 1), products[(n_tiles + 1) % 2], first_column)

    @pl.when(step == n_steps - 1)
    def _():
        top = jnp.max(top_s[...], axis=1, keepdims=True)
        total = jnp.sum(sum_s[...] * jnp.exp2(top_s[...] - top), axis=1, keepdims=True)
        total = top * (1.0 / LOG2E) + jnp.log(total)
        pick = jnp.sum(pick_s[...], axis=1, keepdims=True) * (1.0 / LOG2E)
        both = jnp.where(lane == 0, total, jnp.where(lane == 1, pick, 0.0))
        out_ref[...] = both.T[:2, :]


def vocab_stats(first, row_blocks, degain, row_labels, vocab_all):
    n_rows = row_blocks[0].shape[0]
    n_blocks, width, columns = vocab_all.shape
    tile = 256
    whole = lambda a: pl.BlockSpec(a.shape, lambda j, f: (0, 0), pipeline_mode=pl.Buffered(1))
    kernel = lambda *refs: vocab_kernel(*refs, n_rows=len(row_blocks))
    return pl.pallas_call(
        kernel,
        out_shape=jax.ShapeDtypeStruct((2, n_rows), jnp.float32),
        grid_spec=pltpu.PrefetchScalarGridSpec(
            num_scalar_prefetch=1,
            grid=(n_blocks,),
            in_specs=[
                *(whole(b) for b in row_blocks),
                whole(degain),
                whole(row_labels),
                pl.BlockSpec((1, width, columns), lambda j, f: (j, 0, 0)),
            ],
            out_specs=pl.BlockSpec((2, n_rows), lambda j, f: (0, 0)),
            scratch_shapes=[
                pltpu.VMEM((n_rows, width), jnp.bfloat16),
                *(pltpu.VMEM((tile, columns), jnp.float32) for _ in range(2)),
                *(pltpu.VMEM((n_rows, 128), jnp.float32) for _ in range(4)),
                pltpu.VMEM((n_rows, 128), jnp.int32),
            ],
        ),
        compiler_params=pltpu.CompilerParams(vmem_limit_bytes=VMEM_LIMIT),
        cost_estimate=pl.CostEstimate(
            flops=2 * n_rows * width * n_blocks * columns,
            bytes_accessed=n_rows * width * 2 + n_blocks * width * columns * 2,
            transcendentals=n_rows * n_blocks * columns,
        ),
        name="vocab_stats",
    )(first, *row_blocks, degain, row_labels, vocab_all)


def piece_kernel(row_ref, vocab_ref, piece_ref, sem):
    part = piece_ref.shape[0] // 2
    started = [
        pltpu.make_async_copy(
            vocab_ref.at[pl.ds(pl.multiple_of(row_ref[i] * part, part), part)],
            piece_ref.at[i * part : (i + 1) * part],
            sem.at[i],
        )
        for i in range(2)
    ]
    for copy in started:
        copy.start()
    for copy in started:
        copy.wait()


def vocab_piece(places, w_vocab, part):
    return pl.pallas_call(
        piece_kernel,
        out_shape=jax.ShapeDtypeStruct((2 * part, w_vocab.shape[1]), jnp.bfloat16),
        grid_spec=pltpu.PrefetchScalarGridSpec(
            num_scalar_prefetch=1,
            grid=(),
            in_specs=[pl.BlockSpec(memory_space=pl.ANY)],
            out_specs=pl.BlockSpec(memory_space=pltpu.VMEM),
            scratch_shapes=[pltpu.SemaphoreType.DMA((2,))],
        ),
        compiler_params=pltpu.CompilerParams(vmem_limit_bytes=VMEM_LIMIT),
        cost_estimate=pl.CostEstimate(flops=0, bytes_accessed=2 << 20, transcendentals=0),
        name="vocab_piece",
    )(places, w_vocab)


def split_kernel(w_ref, out_ref):
    part = out_ref.shape[2]
    for i in range(out_ref.shape[0]):
        out_ref[i] = w_ref[:, i * part : (i + 1) * part]


def split_columns(w, n):
    rows, columns = w.shape
    part = columns // n
    return pl.pallas_call(
        split_kernel,
        out_shape=jax.ShapeDtypeStruct((n, rows, part), w.dtype),
        grid=(2,),
        in_specs=[pl.BlockSpec((rows, columns // 2), lambda i: (0, i))],
        out_specs=pl.BlockSpec((n // 2, rows, part), lambda i: (i, 0, 0)),
        cost_estimate=pl.CostEstimate(flops=0, bytes_accessed=4 << 20, transcendentals=0),
        name="split_columns",
    )(w)


def shards(prompts, target_embed, labels, lengths, attn_gain, w_qkv, w_out, final_gain, w_vocab):
    n_prompt = lax.axis_size("prompt")
    n_dp = lax.axis_size("dp")
    n_model = lax.axis_size(MP)
    prompts_here = prompts.shape[0]
    target_len = target_embed.shape[1]
    model_width = target_embed.shape[2]
    vocab_cols = w_vocab.shape[1]
    heads_width = w_out.shape[0]
    z_index = lax.axis_index("mp_0")
    core = lax.axis_index("mp_1")
    part = model_width // n_model
    places = [((z_index + r) % 4) * 2 + (core + k) % 2 for r in RING for k in range(2)]

    place_ids = jnp.stack(places).astype(jnp.int32)
    x_index = lax.axis_index("prompt")
    turn = jnp.where(x_index == 0, 0, jnp.where(x_index == 1, 3, x_index - 1))
    my_pair = ((z_index + turn) % 4) * 2
    pair = jnp.stack([my_pair + core, my_pair + 1 - core]).astype(jnp.int32)
    piece = vocab_piece(pair, w_vocab, part)
    vocab_all = lax.all_gather(piece, ("dp", "prompt"), axis=0, tiled=True)
    vocab_all = vocab_all.reshape(n_dp, model_width, vocab_cols)
    by_part = split_columns(w_out, n_model)
    out_cols = lax.all_to_all(by_part, MP, split_axis=0, concat_axis=0, tiled=True)

    halves = attention(target_embed, prompts, attn_gain, w_qkv)
    contexts = whole_row(*halves)
    halves = output_part(place_ids, contexts, out_cols, target_embed, final_gain)
    row_blocks = whole_row(*halves)

    degain = 1.0 / jnp.concatenate(
        [lax.dynamic_slice_in_dim(final_gain, p * part, part, 0) for p in places], axis=0
    ).reshape(1, -1)
    row_labels = jnp.tile(labels.reshape(-1, 1), (prompts_here, 1))
    first = jnp.stack([lax.axis_index(MP) * vocab_cols, n_model * vocab_cols]).astype(jnp.int32)
    here = vocab_stats(first, row_blocks, degain, row_labels, vocab_all)

    every = of_each(here, MP)
    top_val = jnp.max(every[:, 0], axis=0)
    log_total = top_val + jnp.log(jnp.sum(jnp.exp(every[:, 0] - top_val), axis=0))
    losses = (log_total - jnp.sum(every[:, 1], axis=0)).reshape(prompts_here, 1, target_len)
    valid = jnp.arange(target_len, dtype=jnp.int32)[None, :] < lengths[:, None]
    token_loss = jnp.where(valid[None], losses, 0.0)
    prompt_sums = jnp.sum(token_loss, axis=(1, 2))
    all_prompts = prompts_here * n_prompt
    slot_ids = lax.axis_index("prompt") * prompts_here + jnp.arange(prompts_here, dtype=jnp.int32)
    placed = jnp.sum(
        jnp.where(
            jnp.arange(all_prompts, dtype=jnp.int32)[:, None] == slot_ids[None, :],
            prompt_sums[None, :],
            0.0,
        ),
        axis=1,
    )
    valid_here = jnp.sum(lengths).astype(jnp.float32).reshape(1)
    totals = of_each(jnp.concatenate([placed, valid_here]), ("prompt", "dp"))
    totals = jnp.sum(totals, axis=0)
    prompt_loss = totals[:all_prompts] * float(n_prompt) / totals[all_prompts]
    return (token_loss, prompt_loss)


def solution(mesh):
    finer = Mesh(
        mesh.devices.reshape(mesh.shape["prompt"], mesh.shape["dp"], 4, 2),
        ("prompt", "dp", "mp_0", "mp_1"),
    )
    return jax.shard_map(
        shards,
        mesh=finer,
        in_specs=(
            P("prompt", None, None),
            P("dp", None, None),
            P("dp", None),
            P("dp"),
            P(),
            P(None, None, MP),
            P(MP, None),
            P(),
            P(None, ("dp", "mp_0", "mp_1")),
        ),
        out_specs=(P("prompt", "dp", None), P()),
        check_vma=False,
    )
```

```python
import math

import jax
import jax.numpy as jnp
import numpy as np
from jax import lax
from jax.experimental import pallas as pl
from jax.experimental.pallas import tpu as pltpu
from jax.sharding import Mesh
from jax.sharding import PartitionSpec as P

HD = 128
MP = ("mp_0", "mp_1")
RING = (0, 3, 1, 2)
EPSILON = 1e-05
BASE_THETA = 10000.0
MASKED = -1e30
VMEM_LIMIT = 56 << 20
LOG2E = math.log2(math.e)


def of_each(value, axis):
    copies = jnp.broadcast_to(value, (lax.axis_size(axis), *value.shape))
    return lax.all_to_all(copies, axis, split_axis=0, concat_axis=0, tiled=True)


def shifted(value, axis, shift):
    n = lax.axis_size(axis)
    return lax.ppermute(value, axis, [(i, (i + shift) % n) for i in range(n)])


def ring_pairs(left, right, axis):
    left_before = shifted(left, axis, 1)
    right_after = shifted(right, axis, -1)
    right_before = shifted(right, axis, 1)
    left_after = shifted(left, axis, -1)
    left_far = shifted(left_before, axis, 1)
    right_far = shifted(right_after, axis, -1)
    return [
        (left, right),
        (left_before, right_before),
        (left_after, right_after),
        (left_far, right_far),
    ]


def whole_row(left, right):
    pairs = ring_pairs(left, right, "mp_0")
    return [b for pair in pairs for b in (*pair, *(shifted(half, "mp_1", 1) for half in pair))]


def rope_tables(number_rows, offset):
    positions = np.arange(offset, offset + number_rows, dtype=np.float32)
    indices_f = np.arange(HD // 2, dtype=np.float32)
    frequency = np.exp(indices_f * np.float32(-2.0 * math.log(BASE_THETA) / HD))
    angles = positions[:, None] * frequency[None, :]
    return jnp.asarray(np.cos(angles)), jnp.asarray(np.sin(angles))


def attention_kernel(
    target_ref, prompt_ref, gain_ref, w_ref, cos_t, sin_t, cos_p, sin_p, left_ref, right_ref,
    acc_t, acc_p, sq_t, sq_p, q_s, k_s, v_s, kp_s, vp_s,
):
    step = pl.program_id(0)
    n_prompts = prompt_ref.shape[0]

    @pl.when(step == 0)
    def _():
        acc_t[...] = jnp.zeros_like(acc_t)
        acc_p[...] = jnp.zeros_like(acc_p)
        sq_t[...] = jnp.zeros_like(sq_t)
        sq_p[...] = jnp.zeros_like(sq_p)

    gain = gain_ref[...]

    def lanes_of_squares(x):
        square = x * x
        return sum(square[:, i : i + 128] for i in range(0, square.shape[1], 128))

    x = target_ref[0].astype(jnp.float32)
    sq_t[...] += lanes_of_squares(x)
    scaled = (x * gain).astype(jnp.bfloat16)
    for c in range(3):
        acc_t[c] += jnp.dot(scaled, w_ref[c], preferred_element_type=jnp.float32)
    for p in range(n_prompts):
        x = prompt_ref[p].astype(jnp.float32)
        sq_p[p] += lanes_of_squares(x)
        scaled = (x * gain).astype(jnp.bfloat16)
        for c in range(2):
            acc_p[p, c] += jnp.dot(scaled, w_ref[c + 1], preferred_element_type=jnp.float32)

    @pl.when(step == pl.num_programs(0) - 1)
    def _():
        width = pl.num_programs(0) * target_ref.shape[2]
        heads = q_s.shape[1] // HD

        def inverse(square):
            return lax.rsqrt(jnp.sum(square, axis=1, keepdims=True) / width + EPSILON)

        def turned(values, cos, sin):
            cos = jnp.concatenate([cos, cos], axis=1)
            sin = jnp.concatenate([-sin, sin], axis=1)
            return values * cos + pltpu.roll(values, HD // 2, 1) * sin

        scale_t = inverse(sq_t[...])
        for h in range(heads):
            at = slice(h * HD, (h + 1) * HD)
            q_s[:, at] = turned(acc_t[0, :, at] * scale_t, cos_t[...], sin_t[...]).astype(jnp.bfloat16)
            k_s[:, at] = turned(acc_t[1, :, at] * scale_t, cos_t[...], sin_t[...]).astype(jnp.bfloat16)
            v_s[:, at] = (acc_t[2, :, at] * scale_t).astype(jnp.bfloat16)
            for p in range(n_prompts):
                scale_p = inverse(sq_p[p])
                kp_s[p, :, at] = turned(
                    acc_p[p, 0, :, at] * scale_p, cos_p[...], sin_p[...]
                ).astype(jnp.bfloat16)
                vp_s[p, :, at] = (acc_p[p, 1, :, at] * scale_p).astype(jnp.bfloat16)
        target_len = q_s.shape[0]
        tile = target_len // 2
        transposed = (((1,), (1,)), ((), ()))
        def one_prompt(p, carry):
            for h in range(heads):
                at = slice(h * HD, (h + 1) * HD)
                for first in range(0, target_len, tile):
                    seen = first + tile
                    q = q_s[first:seen, at]
                    near = lax.dot_general(
                        q, kp_s[p, :, at], transposed, preferred_element_type=jnp.float32
                    ) * HD ** (-0.5)
                    own = lax.dot_general(
                        q, k_s[:seen, at], transposed, preferred_element_type=jnp.float32
                    ) * HD ** (-0.5)
                    row = first + lax.broadcasted_iota(jnp.int32, own.shape, 0)
                    key = lax.broadcasted_iota(jnp.int32, own.shape, 1)
                    own = jnp.where(key <= row, own, MASKED)
                    top = jnp.maximum(
                        jnp.max(near, axis=1, keepdims=True), jnp.max(own, axis=1, keepdims=True)
                    )
                    near = jnp.exp(near - top)
                    own = jnp.exp(own - top)
                    norm = 1.0 / (
                        jnp.sum(near, axis=1, keepdims=True) + jnp.sum(own, axis=1, keepdims=True)
                    )
                    context = jnp.dot(
                        (near * norm).astype(jnp.bfloat16),
                        vp_s[p, :, at],
                        preferred_element_type=jnp.float32,
                    ) + jnp.dot(
                        (own * norm).astype(jnp.bfloat16),
                        v_s[:seen, at],
                        preferred_element_type=jnp.float32,
                    )
                    out_ref = (left_ref, right_ref)[h]
                    rows = pl.ds(pl.multiple_of(p * target_len + first, tile), tile)
                    out_ref[rows, :] = context.astype(jnp.bfloat16)
            return carry

        lax.fori_loop(0, n_prompts, one_prompt, 0)


def attention(target_embed, prompts, attn_gain, w_qkv):
    n_prompts, prompt_len, width = prompts.shape
    target_len = target_embed.shape[1]
    inner = w_qkv.shape[2]
    chunk = 1024
    tables = (*rope_tables(target_len, prompt_len), *rope_tables(prompt_len, 0))
    whole = lambda shape: pl.BlockSpec(shape, lambda k: (0,) * len(shape))
    rows = n_prompts * target_len
    return pl.pallas_call(
        attention_kernel,
        out_shape=[jax.ShapeDtypeStruct((rows, inner // 2), jnp.bfloat16)] * 2,
        grid=(width // chunk,),
        in_specs=[
            pl.BlockSpec((1, target_len, chunk), lambda k: (0, 0, k)),
            pl.BlockSpec((n_prompts, prompt_len, chunk), lambda k: (0, 0, k)),
            pl.BlockSpec((1, chunk), lambda k: (0, k)),
            pl.BlockSpec((3, chunk, inner), lambda k: (0, k, 0)),
            *(whole(t.shape) for t in tables),
        ],
        out_specs=[whole((rows, inner // 2))] * 2,
        scratch_shapes=[
            pltpu.VMEM((3, target_len, inner), jnp.float32),
            pltpu.VMEM((n_prompts, 2, prompt_len, inner), jnp.float32),
            pltpu.VMEM((target_len, 128), jnp.float32),
            pltpu.VMEM((n_prompts, prompt_len, 128), jnp.float32),
            *(pltpu.VMEM((target_len, inner), jnp.bfloat16) for _ in range(3)),
            *(pltpu.VMEM((n_prompts, prompt_len, inner), jnp.bfloat16) for _ in range(2)),
        ],
        compiler_params=pltpu.CompilerParams(vmem_limit_bytes=VMEM_LIMIT),
        cost_estimate=pl.CostEstimate(
            flops=8 * 10**9, bytes_accessed=12 * 10**6, transcendentals=2 * 10**6
        ),
        name="attention",
    )(target_embed, prompts, attn_gain.reshape(1, -1), w_qkv, *tables)


def output_kernel(places_ref, *refs):
    *ctx_refs, w_ref, embed_ref, gain_ref, left_ref, right_ref = refs
    total = embed_ref[0].astype(jnp.float32)
    for group in range(w_ref.shape[0]):
        both = jnp.concatenate([ref[...] for ref in ctx_refs[2 * group : 2 * group + 2]], axis=1)
        total += jnp.dot(both, w_ref[places_ref[group]], preferred_element_type=jnp.float32)
    scaled = (total * gain_ref[...]).astype(jnp.bfloat16)
    half = scaled.shape[1] // 2
    left_ref[...] = scaled[:, :half]
    right_ref[...] = scaled[:, half:]


def output_part(places, contexts, out_cols, target_embed, final_gain):
    rows = contexts[0].shape[0]
    part = out_cols.shape[2]
    target_len = target_embed.shape[1]
    tile = target_len // 2
    return pl.pallas_call(
        output_kernel,
        out_shape=[jax.ShapeDtypeStruct((rows, part // 2), jnp.bfloat16)] * 2,
        grid_spec=pltpu.PrefetchScalarGridSpec(
            num_scalar_prefetch=1,
            grid=(rows // tile,),
            in_specs=[
                *(pl.BlockSpec((tile, c.shape[1]), lambda i, at: (i, 0)) for c in contexts),
                pl.BlockSpec(out_cols.shape, lambda i, at: (0, 0, 0)),
                pl.BlockSpec((1, tile, part), lambda i, at: (0, i % 2, at[0])),
                pl.BlockSpec((1, part), lambda i, at: (0, at[0])),
            ],
            out_specs=[pl.BlockSpec((tile, part // 2), lambda i, at: (i, 0))] * 2,
        ),
        compiler_params=pltpu.CompilerParams(vmem_limit_bytes=VMEM_LIMIT),
        cost_estimate=pl.CostEstimate(
            flops=2 * 10**9, bytes_accessed=8 * 10**6, transcendentals=0
        ),
        name="output_part",
    )(places, *contexts, out_cols, target_embed, final_gain.reshape(1, -1))


def vocab_kernel(first_ref, *refs, n_rows):
    row_refs = refs[:n_rows]
    scale_ref, label_ref, w_ref, out_ref = refs[n_rows : n_rows + 4]
    rows_s, first_s, second_s, top_s, sum_s, pick_s, scale_s, label_s = refs[n_rows + 4 :]
    step = pl.program_id(0)
    n_steps = pl.num_programs(0)
    rows = rows_s.shape[0]
    tile, columns = first_s.shape
    n_tiles = rows // tile
    at_tile = lambda t: slice(t * tile, (t + 1) * tile)
    lane = lax.broadcasted_iota(jnp.int32, (1, 128), 1)

    @pl.when(step == 0)
    def _():
        for k, ref in enumerate(row_refs):
            wide = ref.shape[1]
            at = (first_ref[2 + k // 2] * 2 + k % 2) * wide
            rows_s[:, pl.ds(pl.multiple_of(at, wide), wide)] = ref[...]
        scale_s[...] = jnp.broadcast_to(scale_ref[...], scale_s.shape)
        label_s[...] = jnp.broadcast_to(label_ref[...], label_s.shape)
        top_s[...] = jnp.full_like(top_s, MASKED)
        sum_s[...] = jnp.zeros_like(sum_s)
        pick_s[...] = jnp.zeros_like(pick_s)

    def take(at, product_ref, first_column):
        scale = scale_s[at, :]
        logits = [product_ref[:, c : c + 128] * scale for c in range(0, columns, 128)]
        old = top_s[at, :]
        top = old
        for part in logits:
            top = jnp.maximum(top, part)
        total = sum_s[at, :] * jnp.exp2(old - top)
        pick = pick_s[at, :]
        place = label_s[at, :] - (first_column + lane)
        for c, part in enumerate(logits):
            total += jnp.exp2(part - top)
            pick = jnp.where(place == c * 128, part, pick)
        top_s[at, :] = top
        sum_s[at, :] = total
        pick_s[at, :] = pick

    first_column = first_ref[0] + step * first_ref[1]
    products = (first_s, second_s)
    for t in range(n_tiles):
        product = jnp.dot(rows_s[at_tile(t), :], w_ref[0], preferred_element_type=jnp.float32)
        if t:
            take(at_tile(t - 1), products[(t + 1) % 2], first_column)
        products[t % 2][...] = product
    take(at_tile(n_tiles - 1), products[(n_tiles + 1) % 2], first_column)

    @pl.when(step == n_steps - 1)
    def _():
        top = jnp.max(top_s[...], axis=1, keepdims=True)
        total = jnp.sum(sum_s[...] * jnp.exp2(top_s[...] - top), axis=1, keepdims=True)
        total = top * (1.0 / LOG2E) + jnp.log(total)
        pick = jnp.sum(pick_s[...], axis=1, keepdims=True) * (1.0 / LOG2E)
        both = jnp.where(lane == 0, total, jnp.where(lane == 1, pick, 0.0))
        out_ref[...] = both.T[:2, :]


def vocab_stats(first, row_blocks, scale, row_labels, vocab_all):
    n_rows = row_blocks[0].shape[0]
    n_blocks, width, columns = vocab_all.shape
    tile = 256
    whole = lambda a: pl.BlockSpec(a.shape, lambda j, f: (0, 0), pipeline_mode=pl.Buffered(1))
    kernel = lambda *refs: vocab_kernel(*refs, n_rows=len(row_blocks))
    return pl.pallas_call(
        kernel,
        out_shape=jax.ShapeDtypeStruct((2, n_rows), jnp.float32),
        grid_spec=pltpu.PrefetchScalarGridSpec(
            num_scalar_prefetch=1,
            grid=(n_blocks,),
            in_specs=[
                *(whole(b) for b in row_blocks),
                whole(scale),
                whole(row_labels),
                pl.BlockSpec((1, width, columns), lambda j, f: (j, 0, 0)),
            ],
            out_specs=pl.BlockSpec((2, n_rows), lambda j, f: (0, 0)),
            scratch_shapes=[
                pltpu.VMEM((n_rows, width), jnp.bfloat16),
                *(pltpu.VMEM((tile, columns), jnp.float32) for _ in range(2)),
                *(pltpu.VMEM((n_rows, 128), jnp.float32) for _ in range(4)),
                pltpu.VMEM((n_rows, 128), jnp.int32),
            ],
        ),
        compiler_params=pltpu.CompilerParams(vmem_limit_bytes=VMEM_LIMIT),
        cost_estimate=pl.CostEstimate(
            flops=2 * n_rows * width * n_blocks * columns,
            bytes_accessed=n_rows * width * 2 + n_blocks * width * columns * 2,
            transcendentals=n_rows * n_blocks * columns,
        ),
        name="vocab_stats",
    )(first, *row_blocks, scale, row_labels, vocab_all)


def split_kernel(w_ref, out_ref):
    part = out_ref.shape[2]
    for i in range(out_ref.shape[0]):
        out_ref[i] = w_ref[:, i * part : (i + 1) * part]


def split_columns(w, n):
    rows, columns = w.shape
    part = columns // n
    return pl.pallas_call(
        split_kernel,
        out_shape=jax.ShapeDtypeStruct((n, rows, part), w.dtype),
        grid=(2,),
        in_specs=[pl.BlockSpec((rows, columns // 2), lambda i: (0, i))],
        out_specs=pl.BlockSpec((n // 2, rows, part), lambda i: (i, 0, 0)),
        cost_estimate=pl.CostEstimate(flops=0, bytes_accessed=4 << 20, transcendentals=0),
        name="split_columns",
    )(w)


def shards(prompts, target_embed, labels, lengths, attn_gain, w_qkv, w_out, final_gain, w_vocab):
    n_prompt = lax.axis_size("prompt")
    n_dp = lax.axis_size("dp")
    n_model = lax.axis_size(MP)
    prompts_here = prompts.shape[0]
    target_len = target_embed.shape[1]
    model_width = target_embed.shape[2]
    vocab_cols = w_vocab.shape[1]
    heads_width = w_out.shape[0]
    z_index = lax.axis_index("mp_0")
    core = lax.axis_index("mp_1")
    part = model_width // n_model
    places = [((z_index + r) % 4) * 2 + (core + k) % 2 for r in RING for k in range(2)]

    place_ids = jnp.stack(places).astype(jnp.int32)
    share = model_width // n_prompt
    piece = lax.dynamic_slice_in_dim(w_vocab, lax.axis_index("prompt") * share, share, 0)
    vocab_all = lax.all_gather(piece, ("dp", "prompt"), axis=0, tiled=True)
    vocab_all = vocab_all.reshape(n_dp, model_width, vocab_cols)
    by_part = split_columns(w_out, n_model)
    out_cols = lax.all_to_all(by_part, MP, split_axis=0, concat_axis=0, tiled=True)

    halves = attention(target_embed, prompts, attn_gain, w_qkv)
    contexts = whole_row(*halves)
    halves = output_part(place_ids, contexts, out_cols, target_embed, final_gain)
    row_blocks = whole_row(*halves)

    squares = 0.0
    for k, block in enumerate(row_blocks):
        wide = block.shape[1]
        gain = lax.dynamic_slice_in_dim(final_gain, (places[k // 2] * 2 + k % 2) * wide, wide, 0)
        unscaled = block.astype(jnp.float32) / gain
        squares = squares + jnp.sum(unscaled * unscaled, axis=1, keepdims=True)
    scale = lax.rsqrt(squares / model_width + EPSILON) * LOG2E
    row_labels = jnp.tile(labels.reshape(-1, 1), (prompts_here, 1))
    first = [lax.axis_index(MP) * vocab_cols, n_model * vocab_cols, *places]
    first = jnp.stack(first).astype(jnp.int32)
    here = vocab_stats(first, row_blocks, scale, row_labels, vocab_all)

    every = of_each(here, MP)
    top_val = jnp.max(every[:, 0], axis=0)
    log_total = top_val + jnp.log(jnp.sum(jnp.exp(every[:, 0] - top_val), axis=0))
    losses = (log_total - jnp.sum(every[:, 1], axis=0)).reshape(prompts_here, 1, target_len)
    valid = jnp.arange(target_len, dtype=jnp.int32)[None, :] < lengths[:, None]
    token_loss = jnp.where(valid[None], losses, 0.0)
    prompt_sums = jnp.sum(token_loss, axis=(1, 2))
    all_prompts = prompts_here * n_prompt
    slot_ids = lax.axis_index("prompt") * prompts_here + jnp.arange(prompts_here, dtype=jnp.int32)
    placed = jnp.sum(
        jnp.where(
            jnp.arange(all_prompts, dtype=jnp.int32)[:, None] == slot_ids[None, :],
            prompt_sums[None, :],
            0.0,
        ),
        axis=1,
    )
    valid_here = jnp.sum(lengths).astype(jnp.float32).reshape(1)
    totals = of_each(jnp.concatenate([placed, valid_here]), ("prompt", "dp"))
    totals = jnp.sum(totals, axis=0)
    prompt_loss = totals[:all_prompts] * float(n_prompt) / totals[all_prompts]
    return (token_loss, prompt_loss)


def solution(mesh):
    finer = Mesh(
        mesh.devices.reshape(mesh.shape["prompt"], mesh.shape["dp"], 4, 2),
        ("prompt", "dp", "mp_0", "mp_1"),
    )
    return jax.shard_map(
        shards,
        mesh=finer,
        in_specs=(
            P("prompt", None, None),
            P("dp", None, None),
            P("dp", None),
            P("dp"),
            P(),
            P(None, None, MP),
            P(MP, None),
            P(),
            P(None, ("dp", "mp_0", "mp_1")),
        ),
        out_specs=(P("prompt", "dp", None), P()),
        check_vma=False,
    )
```

```python
import math

import jax
import jax.numpy as jnp
import numpy as np
from jax import lax
from jax.experimental import pallas as pl
from jax.experimental.pallas import tpu as pltpu
from jax.sharding import Mesh
from jax.sharding import PartitionSpec as P

HD = 128
MP = ("mp_0", "mp_1")
RING = (0, 3, 1, 2)
EPSILON = 1e-05
BASE_THETA = 10000.0
MASKED = -1e30
VMEM_LIMIT = 56 << 20
LOG2E = math.log2(math.e)


def of_each(value, axis):
    copies = jnp.broadcast_to(value, (lax.axis_size(axis), *value.shape))
    return lax.all_to_all(copies, axis, split_axis=0, concat_axis=0, tiled=True)


def shifted(value, axis, shift):
    n = lax.axis_size(axis)
    return lax.ppermute(value, axis, [(i, (i + shift) % n) for i in range(n)])


def ring_pairs(left, right, axis):
    left_before = shifted(left, axis, 1)
    right_after = shifted(right, axis, -1)
    right_before = shifted(right, axis, 1)
    left_after = shifted(left, axis, -1)
    left_far = shifted(left_before, axis, 1)
    right_far = shifted(right_after, axis, -1)
    return [
        (left, right),
        (left_before, right_before),
        (left_after, right_after),
        (left_far, right_far),
    ]


def whole_row(left, right):
    pairs = ring_pairs(left, right, "mp_0")
    return [b for pair in pairs for b in (*pair, *(shifted(half, "mp_1", 1) for half in pair))]


def rope_tables(number_rows, offset):
    positions = np.arange(offset, offset + number_rows, dtype=np.float32)
    indices_f = np.arange(HD // 2, dtype=np.float32)
    frequency = np.exp(indices_f * np.float32(-2.0 * math.log(BASE_THETA) / HD))
    angles = positions[:, None] * frequency[None, :]
    return jnp.asarray(np.cos(angles)), jnp.asarray(np.sin(angles))


def attention_kernel(
    target_ref, prompt_ref, gain_ref, w_ref, cos_t, sin_t, cos_p, sin_p, left_ref, right_ref,
    acc_t, acc_p, sq_t, sq_p, q_s, k_s, v_s, kp_s, vp_s,
):
    step = pl.program_id(0)
    n_prompts = prompt_ref.shape[0]

    @pl.when(step == 0)
    def _():
        acc_t[...] = jnp.zeros_like(acc_t)
        acc_p[...] = jnp.zeros_like(acc_p)
        sq_t[...] = jnp.zeros_like(sq_t)
        sq_p[...] = jnp.zeros_like(sq_p)

    gain = gain_ref[...]

    def lanes_of_squares(x):
        square = x * x
        return sum(square[:, i : i + 128] for i in range(0, square.shape[1], 128))

    x = target_ref[0].astype(jnp.float32)
    sq_t[...] += lanes_of_squares(x)
    scaled = (x * gain).astype(jnp.bfloat16)
    for c in range(3):
        acc_t[c] += jnp.dot(scaled, w_ref[c], preferred_element_type=jnp.float32)
    for p in range(n_prompts):
        x = prompt_ref[p].astype(jnp.float32)
        sq_p[p] += lanes_of_squares(x)
        scaled = (x * gain).astype(jnp.bfloat16)
        for c in range(2):
            acc_p[p, c] += jnp.dot(scaled, w_ref[c + 1], preferred_element_type=jnp.float32)

    @pl.when(step == pl.num_programs(0) - 1)
    def _():
        width = pl.num_programs(0) * target_ref.shape[2]
        heads = q_s.shape[1] // HD

        def inverse(square):
            return lax.rsqrt(jnp.sum(square, axis=1, keepdims=True) / width + EPSILON)

        def turned(values, cos, sin):
            cos = jnp.concatenate([cos, cos], axis=1)
            sin = jnp.concatenate([-sin, sin], axis=1)
            return values * cos + pltpu.roll(values, HD // 2, 1) * sin

        scale_t = inverse(sq_t[...])
        for h in range(heads):
            at = slice(h * HD, (h + 1) * HD)
            q_s[:, at] = turned(acc_t[0, :, at] * scale_t, cos_t[...], sin_t[...]).astype(jnp.bfloat16)
            k_s[:, at] = turned(acc_t[1, :, at] * scale_t, cos_t[...], sin_t[...]).astype(jnp.bfloat16)
            v_s[:, at] = (acc_t[2, :, at] * scale_t).astype(jnp.bfloat16)
            for p in range(n_prompts):
                scale_p = inverse(sq_p[p])
                kp_s[p, :, at] = turned(
                    acc_p[p, 0, :, at] * scale_p, cos_p[...], sin_p[...]
                ).astype(jnp.bfloat16)
                vp_s[p, :, at] = (acc_p[p, 1, :, at] * scale_p).astype(jnp.bfloat16)
        target_len = q_s.shape[0]
        tile = target_len // 2
        transposed = (((1,), (1,)), ((), ()))
        def one_prompt(p, carry):
            for h in range(heads):
                at = slice(h * HD, (h + 1) * HD)
                for first in range(0, target_len, tile):
                    seen = first + tile
                    q = q_s[first:seen, at]
                    near = lax.dot_general(
                        q, kp_s[p, :, at], transposed, preferred_element_type=jnp.float32
                    ) * HD ** (-0.5)
                    own = lax.dot_general(
                        q, k_s[:seen, at], transposed, preferred_element_type=jnp.float32
                    ) * HD ** (-0.5)
                    row = first + lax.broadcasted_iota(jnp.int32, own.shape, 0)
                    key = lax.broadcasted_iota(jnp.int32, own.shape, 1)
                    own = jnp.where(key <= row, own, MASKED)
                    top = jnp.maximum(
                        jnp.max(near, axis=1, keepdims=True), jnp.max(own, axis=1, keepdims=True)
                    )
                    near = jnp.exp(near - top)
                    own = jnp.exp(own - top)
                    norm = 1.0 / (
                        jnp.sum(near, axis=1, keepdims=True) + jnp.sum(own, axis=1, keepdims=True)
                    )
                    context = jnp.dot(
                        (near * norm).astype(jnp.bfloat16),
                        vp_s[p, :, at],
                        preferred_element_type=jnp.float32,
                    ) + jnp.dot(
                        (own * norm).astype(jnp.bfloat16),
                        v_s[:seen, at],
                        preferred_element_type=jnp.float32,
                    )
                    out_ref = (left_ref, right_ref)[h]
                    rows = pl.ds(pl.multiple_of(p * target_len + first, tile), tile)
                    out_ref[rows, :] = context.astype(jnp.bfloat16)
            return carry

        lax.fori_loop(0, n_prompts, one_prompt, 0)


def attention(target_embed, prompts, attn_gain, w_qkv):
    n_prompts, prompt_len, width = prompts.shape
    target_len = target_embed.shape[1]
    inner = w_qkv.shape[2]
    chunk = 1024
    tables = (*rope_tables(target_len, prompt_len), *rope_tables(prompt_len, 0))
    whole = lambda shape: pl.BlockSpec(shape, lambda k: (0,) * len(shape))
    rows = n_prompts * target_len
    return pl.pallas_call(
        attention_kernel,
        out_shape=[jax.ShapeDtypeStruct((rows, inner // 2), jnp.bfloat16)] * 2,
        grid=(width // chunk,),
        in_specs=[
            pl.BlockSpec((1, target_len, chunk), lambda k: (0, 0, k)),
            pl.BlockSpec((n_prompts, prompt_len, chunk), lambda k: (0, 0, k)),
            pl.BlockSpec((1, chunk), lambda k: (0, k)),
            pl.BlockSpec((3, chunk, inner), lambda k: (0, k, 0)),
            *(whole(t.shape) for t in tables),
        ],
        out_specs=[whole((rows, inner // 2))] * 2,
        scratch_shapes=[
            pltpu.VMEM((3, target_len, inner), jnp.float32),
            pltpu.VMEM((n_prompts, 2, prompt_len, inner), jnp.float32),
            pltpu.VMEM((target_len, 128), jnp.float32),
            pltpu.VMEM((n_prompts, prompt_len, 128), jnp.float32),
            *(pltpu.VMEM((target_len, inner), jnp.bfloat16) for _ in range(3)),
            *(pltpu.VMEM((n_prompts, prompt_len, inner), jnp.bfloat16) for _ in range(2)),
        ],
        compiler_params=pltpu.CompilerParams(vmem_limit_bytes=VMEM_LIMIT),
        cost_estimate=pl.CostEstimate(
            flops=8 * 10**9, bytes_accessed=12 * 10**6, transcendentals=2 * 10**6
        ),
        name="attention",
    )(target_embed, prompts, attn_gain.reshape(1, -1), w_qkv, *tables)


def output_kernel(places_ref, *refs):
    *ctx_refs, w_ref, embed_ref, gain_ref, left_ref, right_ref = refs
    total = embed_ref[0].astype(jnp.float32)
    for group in range(w_ref.shape[0]):
        both = jnp.concatenate([ref[...] for ref in ctx_refs[2 * group : 2 * group + 2]], axis=1)
        total += jnp.dot(both, w_ref[places_ref[group]], preferred_element_type=jnp.float32)
    scaled = (total * gain_ref[...]).astype(jnp.bfloat16)
    half = scaled.shape[1] // 2
    left_ref[...] = scaled[:, :half]
    right_ref[...] = scaled[:, half:]


def output_part(places, contexts, out_cols, target_embed, final_gain):
    rows = contexts[0].shape[0]
    part = out_cols.shape[2]
    target_len = target_embed.shape[1]
    tile = target_len // 2
    return pl.pallas_call(
        output_kernel,
        out_shape=[jax.ShapeDtypeStruct((rows, part // 2), jnp.bfloat16)] * 2,
        grid_spec=pltpu.PrefetchScalarGridSpec(
            num_scalar_prefetch=1,
            grid=(rows // tile,),
            in_specs=[
                *(pl.BlockSpec((tile, c.shape[1]), lambda i, at: (i, 0)) for c in contexts),
                pl.BlockSpec(out_cols.shape, lambda i, at: (0, 0, 0)),
                pl.BlockSpec((1, tile, part), lambda i, at: (0, i % 2, at[0])),
                pl.BlockSpec((1, part), lambda i, at: (0, at[0])),
            ],
            out_specs=[pl.BlockSpec((tile, part // 2), lambda i, at: (i, 0))] * 2,
        ),
        compiler_params=pltpu.CompilerParams(vmem_limit_bytes=VMEM_LIMIT),
        cost_estimate=pl.CostEstimate(
            flops=2 * 10**9, bytes_accessed=8 * 10**6, transcendentals=0
        ),
        name="output_part",
    )(places, *contexts, out_cols, target_embed, final_gain.reshape(1, -1))


def vocab_kernel(first_ref, *refs, n_rows):
    row_refs = refs[:n_rows]
    scale_ref, label_ref, w_ref, out_ref = refs[n_rows : n_rows + 4]
    rows_s, first_s, second_s, top_s, sum_s, pick_s, scale_s, label_s = refs[n_rows + 4 :]
    step = pl.program_id(0)
    n_steps = pl.num_programs(0)
    rows = rows_s.shape[0]
    tile, columns = first_s.shape
    n_tiles = rows // tile
    at_tile = lambda t: slice(t * tile, (t + 1) * tile)
    lane = lax.broadcasted_iota(jnp.int32, (1, 128), 1)

    @pl.when(step == 0)
    def _():
        for k, ref in enumerate(row_refs):
            wide = ref.shape[1]
            at = (first_ref[2 + k // 2] * 2 + k % 2) * wide
            rows_s[:, pl.ds(pl.multiple_of(at, wide), wide)] = ref[...]
        scale_s[...] = jnp.broadcast_to(scale_ref[...], scale_s.shape)
        label_s[...] = jnp.broadcast_to(label_ref[...], label_s.shape)
        top_s[...] = jnp.full_like(top_s, MASKED)
        sum_s[...] = jnp.zeros_like(sum_s)
        pick_s[...] = jnp.zeros_like(pick_s)

    def take(at, product_ref, first_column):
        scale = scale_s[at, :]
        logits = [product_ref[:, c : c + 128] * scale for c in range(0, columns, 128)]
        old = top_s[at, :]
        top = old
        for part in logits:
            top = jnp.maximum(top, part)
        total = sum_s[at, :] * jnp.exp2(old - top)
        pick = pick_s[at, :]
        place = label_s[at, :] - (first_column + lane)
        for c, part in enumerate(logits):
            total += jnp.exp2(part - top)
            pick = jnp.where(place == c * 128, part, pick)
        top_s[at, :] = top
        sum_s[at, :] = total
        pick_s[at, :] = pick

    first_column = first_ref[0] + step * first_ref[1]
    products = (first_s, second_s)
    for t in range(n_tiles):
        product = jnp.dot(rows_s[at_tile(t), :], w_ref[0], preferred_element_type=jnp.float32)
        if t:
            take(at_tile(t - 1), products[(t + 1) % 2], first_column)
        products[t % 2][...] = product
    take(at_tile(n_tiles - 1), products[(n_tiles + 1) % 2], first_column)

    @pl.when(step == n_steps - 1)
    def _():
        top = jnp.max(top_s[...], axis=1, keepdims=True)
        total = jnp.sum(sum_s[...] * jnp.exp2(top_s[...] - top), axis=1, keepdims=True)
        total = top * (1.0 / LOG2E) + jnp.log(total)
        pick = jnp.sum(pick_s[...], axis=1, keepdims=True) * (1.0 / LOG2E)
        both = jnp.where(lane == 0, total, jnp.where(lane == 1, pick, 0.0))
        out_ref[...] = jnp.broadcast_to(both.T[None, :2, :], out_ref.shape)


def vocab_stats(first, row_blocks, scale, row_labels, vocab_all, n_copies):
    n_rows = row_blocks[0].shape[0]
    n_blocks, width, columns = vocab_all.shape
    tile = 256
    whole = lambda a: pl.BlockSpec(a.shape, lambda j, f: (0, 0), pipeline_mode=pl.Buffered(1))
    kernel = lambda *refs: vocab_kernel(*refs, n_rows=len(row_blocks))
    return pl.pallas_call(
        kernel,
        out_shape=jax.ShapeDtypeStruct((n_copies, 2, n_rows), jnp.float32),
        grid_spec=pltpu.PrefetchScalarGridSpec(
            num_scalar_prefetch=1,
            grid=(n_blocks,),
            in_specs=[
                *(whole(b) for b in row_blocks),
                whole(scale),
                whole(row_labels),
                pl.BlockSpec((1, width, columns), lambda j, f: (j, 0, 0)),
            ],
            out_specs=pl.BlockSpec((n_copies, 2, n_rows), lambda j, f: (0, 0, 0)),
            scratch_shapes=[
                pltpu.VMEM((n_rows, width), jnp.bfloat16),
                *(pltpu.VMEM((tile, columns), jnp.float32) for _ in range(2)),
                *(pltpu.VMEM((n_rows, 128), jnp.float32) for _ in range(4)),
                pltpu.VMEM((n_rows, 128), jnp.int32),
            ],
        ),
        compiler_params=pltpu.CompilerParams(vmem_limit_bytes=VMEM_LIMIT),
        cost_estimate=pl.CostEstimate(
            flops=2 * n_rows * width * n_blocks * columns,
            bytes_accessed=n_rows * width * 2 + n_blocks * width * columns * 2,
            transcendentals=n_rows * n_blocks * columns,
        ),
        name="vocab_stats",
    )(first, *row_blocks, scale, row_labels, vocab_all)


def split_kernel(w_ref, out_ref):
    part = out_ref.shape[2]
    for i in range(out_ref.shape[0]):
        out_ref[i] = w_ref[:, i * part : (i + 1) * part]


def split_columns(w, n):
    rows, columns = w.shape
    part = columns // n
    return pl.pallas_call(
        split_kernel,
        out_shape=jax.ShapeDtypeStruct((n, rows, part), w.dtype),
        grid=(2,),
        in_specs=[pl.BlockSpec((rows, columns // 2), lambda i: (0, i))],
        out_specs=pl.BlockSpec((n // 2, rows, part), lambda i: (i, 0, 0)),
        cost_estimate=pl.CostEstimate(flops=0, bytes_accessed=4 << 20, transcendentals=0),
        name="split_columns",
    )(w)


def shards(prompts, target_embed, labels, lengths, attn_gain, w_qkv, w_out, final_gain, w_vocab):
    n_prompt = lax.axis_size("prompt")
    n_dp = lax.axis_size("dp")
    n_model = lax.axis_size(MP)
    prompts_here = prompts.shape[0]
    target_len = target_embed.shape[1]
    model_width = target_embed.shape[2]
    vocab_cols = w_vocab.shape[1]
    heads_width = w_out.shape[0]
    z_index = lax.axis_index("mp_0")
    core = lax.axis_index("mp_1")
    part = model_width // n_model
    places = [((z_index + r) % 4) * 2 + (core + k) % 2 for r in RING for k in range(2)]

    place_ids = jnp.stack(places).astype(jnp.int32)
    share = model_width // n_prompt
    piece = lax.dynamic_slice_in_dim(w_vocab, lax.axis_index("prompt") * share, share, 0)
    vocab_all = lax.all_gather(piece, ("dp", "prompt"), axis=0, tiled=True)
    vocab_all = vocab_all.reshape(n_dp, model_width, vocab_cols)
    by_part = split_columns(w_out, n_model)
    out_cols = lax.all_to_all(by_part, MP, split_axis=0, concat_axis=0, tiled=True)

    halves = attention(target_embed, prompts, attn_gain, w_qkv)
    contexts = whole_row(*halves)
    halves = output_part(place_ids, contexts, out_cols, target_embed, final_gain)
    row_blocks = whole_row(*halves)

    squares = 0.0
    for k, block in enumerate(row_blocks):
        wide = block.shape[1]
        gain = lax.dynamic_slice_in_dim(final_gain, (places[k // 2] * 2 + k % 2) * wide, wide, 0)
        unscaled = block.astype(jnp.float32) / gain
        squares = squares + jnp.sum(unscaled * unscaled, axis=1, keepdims=True)
    scale = lax.rsqrt(squares / model_width + EPSILON) * LOG2E
    row_labels = jnp.tile(labels.reshape(-1, 1), (prompts_here, 1))
    first = [lax.axis_index(MP) * vocab_cols, n_model * vocab_cols, *places]
    first = jnp.stack(first).astype(jnp.int32)
    here = vocab_stats(first, row_blocks, scale, row_labels, vocab_all, n_model)

    every = lax.all_to_all(here, MP, split_axis=0, concat_axis=0, tiled=True)
    top_val = jnp.max(every[:, 0], axis=0)
    log_total = top_val + jnp.log(jnp.sum(jnp.exp(every[:, 0] - top_val), axis=0))
    losses = (log_total - jnp.sum(every[:, 1], axis=0)).reshape(prompts_here, 1, target_len)
    valid = jnp.arange(target_len, dtype=jnp.int32)[None, :] < lengths[:, None]
    token_loss = jnp.where(valid[None], losses, 0.0)
    prompt_sums = jnp.sum(token_loss, axis=(1, 2))
    all_prompts = prompts_here * n_prompt
    slot_ids = lax.axis_index("prompt") * prompts_here + jnp.arange(prompts_here, dtype=jnp.int32)
    placed = jnp.sum(
        jnp.where(
            jnp.arange(all_prompts, dtype=jnp.int32)[:, None] == slot_ids[None, :],
            prompt_sums[None, :],
            0.0,
        ),
        axis=1,
    )
    valid_here = jnp.sum(lengths).astype(jnp.float32).reshape(1)
    totals = of_each(jnp.concatenate([placed, valid_here]), ("prompt", "dp"))
    totals = jnp.sum(totals, axis=0)
    prompt_loss = totals[:all_prompts] * float(n_prompt) / totals[all_prompts]
    return (token_loss, prompt_loss)


def solution(mesh):
    finer = Mesh(
        mesh.devices.reshape(mesh.shape["prompt"], mesh.shape["dp"], 4, 2),
        ("prompt", "dp", "mp_0", "mp_1"),
    )
    return jax.shard_map(
        shards,
        mesh=finer,
        in_specs=(
            P("prompt", None, None),
            P("dp", None, None),
            P("dp", None),
            P("dp"),
            P(),
            P(None, None, MP),
            P(MP, None),
            P(),
            P(None, ("dp", "mp_0", "mp_1")),
        ),
        out_specs=(P("prompt", "dp", None), P()),
        check_vma=False,
    )
```
